32 devices in a mesh: passage: 2 (over x), brick: 16 (over z, y, core).
Axes of the slice: x: 2, y: 2, z: 4, core: 2. Of those that a mesh axis runs over, the one named last changes fastest.
Arguments:
- jac_blocks: bfloat16 [2, 25, 16, 8192], P('passage', None, None, 'brick'), may hold values from -6 to 6
- psi_start: float32 [2, 10, 16, 64, 128], P('passage', None, 'brick'), may hold values from -6 to 6
- source: float32 [2, 10, 16, 64, 128], P('passage', None, 'brick'), may hold values from -6 to 6
- pseudo_step: float32 [2, 16, 64, 128], P('passage', 'brick'), may hold values from 0.1 to 0.4
- dissipation: float32 [2, 16, 64, 128], P('passage', 'brick'), may hold values from 0.04 to 0.15
- freq_volume: float32 [2, 16, 64, 128], P('passage', 'brick'), may hold values from 0.2 to 2
- normals: float32 [2, 3, 16, 64], P('passage', None, 'brick'), may hold values from -6 to 6
- face_owner: int32 [2, 1024, 1], P('passage', 'brick'), may hold values from 0 to 15; in each aligned block of 64 rows (0 to 63, 64 to 127, ..., all dimensions but the last counted through in order) at most 16 rows name the same one
- face_slot: int32 [2, 1024], P('passage', 'brick'), may hold values from 0 to 255
Outputs:
- adjoint: float32 [2, 10, 16, 64, 128], P('passage', None, 'brick')
- sensitivity: float32 [2, 6, 4096], P('passage', None, 'brick')
The draws below stay inside these ranges and needn't reach their ends.
Inputs may be any that keep to these rules, and one draw needn't show every extreme that they name: `face_owner`: in the 64 faces of one device (aligned blocks of the rows), no brick is named by more than 16 faces, and in some block some brick is named by exactly 16.
All inputs are finite; a program needn't handle non-finite values.
Results may differ from the reference program's by a relative error of at most 0.0003.
Values may be sent and summed in bfloat16 or wider, within the bound.
A program may use at most 64 MiB of HBM per device.

```python
import math
import jax
import jax.numpy as jnp
import numpy as np

PASSAGES = 2
CI = 1
NJ = 64
NK = 128
NI = 16
NJK = 8192
NODE_DEV = 256
NODES = 4096
CAP = 16
SWEEPS = 2
ND = 1
BLADES = 36
N_BRICK = 16


def plant(array, stream_key, least, largest):
    dims = array.shape
    spot = [jax.random.randint(jax.random.fold_in(stream_key, axis), (), 0, dims[axis]) for axis in range(len(dims))]
    array = array.at[tuple(spot)].set(least)
    longest = dims.index(max(dims))
    spot[longest] = (spot[longest] + 1) % dims[longest]
    return array.at[tuple(spot)].set(largest)


def block_levels(own_key, extent, shards, smallest, largest):
    def one(axis_at, blocks):
        steps = jax.random.uniform(jax.random.fold_in(jax.random.fold_in(own_key, 6), axis_at), (blocks,), jnp.float32, smallest / len(shards), largest / len(shards))
        return jnp.repeat(jnp.exp(steps), extent[axis_at] // blocks).reshape((-1,) + (1,) * (len(extent) - axis_at - 1))

    level = one(*shards[0])
    for cut in shards[1:]:
        level = level * one(*cut)
    return level


def routed_block(key, own, number, rows, number_of, top, most, slope):
    sequence = jax.random.permutation(key, number_of)
    crowded, ordinary = shares(number_of, rows * top, most, slope, True), shares(number_of, rows * top, most, slope, False)
    places = jnp.arange(number_of)

    def named(sizes, turn):
        used = int((sizes > 0).sum())
        fixed = max(1, used // 4)
        shifted = fixed + (places - fixed + turn * (used - fixed)) % max(1, number_of - fixed)
        return jnp.zeros((number_of,), jnp.int32).at[sequence[jnp.where(places < fixed, places, shifted)]].set(jnp.asarray(sizes, jnp.int32))

    sizes = jnp.where(number % 4 == 0, named(crowded, number // 4), named(ordinary, number - number // 4 - 1))
    mixed = jax.random.permutation(jax.random.fold_in(own, 3), number_of)
    donor, sink = mixed[0:number_of // 2 * 2:2], mixed[1:number_of // 2 * 2:2]
    slack = jnp.minimum(sizes[donor] - 1, most - sizes[sink]) // 2
    slack = jnp.where((donor == sequence[0]) | (sink == sequence[0]) | (sizes[sink] == 0), 0, jnp.maximum(slack, 0))
    shifted = jax.random.randint(jax.random.fold_in(own, 4), (number_of // 2,), 0, 1 << 20) % (slack + 1)
    sizes = sizes.at[donor].add(-shifted).at[sink].add(shifted)
    members = jnp.searchsorted(jnp.cumsum(sizes), jnp.arange(rows * top), side="right").astype(jnp.int32)
    table = members.reshape(top, rows).T
    table = table[jax.random.permutation(jax.random.fold_in(own, 1), rows)]
    turn = jax.random.randint(jax.random.fold_in(own, 2), (rows, 1), 0, top)
    return jnp.take_along_axis(table, (jnp.arange(top)[None, :] + turn) % top, axis=1)


def shares(count, total, most, skew, full):
    loads = [(1 << 20) // math.isqrt(rank ** skew) + 1 for rank in range(1, count + 1)]
    largest = most if full else min(most, max(-(-total // count), total * loads[0] // sum(loads)))
    least = 1 if total - largest >= count - 1 else 0
    counts, rest = [largest] + [least] * (count - 1), total - largest - least * (count - 1)
    while rest > 0:
        candidates = [i for i in range(1, count) if counts[i] < largest] or [i for i in range(1, count) if counts[i] < most]
        mass, budget = sum([loads[i] for i in candidates]), rest
        for i in candidates:
            more = min(most - counts[i], max(1, budget * loads[i] // mass), rest)
            counts[i] = counts[i] + more
            rest = rest - more
    return np.array(counts)


def noise(key, shape, spread, limit, shards=(), dtype=jnp.bfloat16):
    values = spread * jax.random.normal(key, shape, jnp.float32)
    if shards:
        values = values * block_levels(key, shape, shards, -0.22, 0.18)
    return jnp.clip(values, -limit, limit).astype(dtype)


def setup_inputs(seed: int = 0) -> dict:
    seeds = jax.random.split(jax.random.key(seed), 10)
    jac_blocks = noise(seeds[0], (PASSAGES, 25, NI, NJK), 0.4, 6.0, ((0, 2), (3, 16)))
    psi_start = noise(seeds[1], (PASSAGES, 10, NI, NJ, NK), 1.0, 6.0, ((0, 2), (2, 16)), jnp.float32)
    source = noise(seeds[2], (PASSAGES, 10, NI, NJ, NK), 1.0, 6.0, ((0, 2), (2, 16)), jnp.float32)
    pseudo_step = jnp.clip(jnp.exp(math.log(0.4) - 1.3862944 * jax.random.uniform(seeds[3], (PASSAGES, NI, NJ, NK), jnp.float32) ** block_levels(seeds[3], (PASSAGES, NI, NJ, NK), ((0, 2), (1, 16)), -0.2, 0.2)), 0.1, 0.4)
    dissipation = jnp.clip(jnp.exp(math.log(0.15) - 1.3217559 * jax.random.uniform(seeds[4], (PASSAGES, NI, NJ, NK), jnp.float32) ** block_levels(seeds[4], (PASSAGES, NI, NJ, NK), ((0, 2), (1, 16)), -0.2, 0.2)), 0.04, 0.15)
    freq_volume = jnp.clip(jnp.exp(math.log(2.0) - 2.3025851 * jax.random.uniform(seeds[5], (PASSAGES, NI, NJ, NK), jnp.float32) ** block_levels(seeds[5], (PASSAGES, NI, NJ, NK), ((0, 2), (1, 16)), -0.2, 0.2)), 0.2, 2.0)
    normals = noise(seeds[6], (PASSAGES, 3, NI, NJ), 1.0, 6.0, ((0, 2), (2, 16)), jnp.float32)
    face_owner_keys = jax.random.split(jax.random.fold_in(seeds[7], 1), PASSAGES * (NI * NJ) // (CI * NJ))
    face_owner_turns = jax.random.permutation(jax.random.fold_in(seeds[7], 3), PASSAGES * (NI * NJ) // (CI * NJ))
    face_owner = jax.vmap(lambda own, number: routed_block(jax.random.fold_in(seeds[7], 2), own, number, CI * NJ, N_BRICK, 1, CAP, 2))(face_owner_keys, face_owner_turns).reshape((PASSAGES, NI * NJ, 1))
    face_slot = plant(jax.random.randint(seeds[8], (PASSAGES, NI * NJ), 0, NODE_DEV), jax.random.fold_in(seeds[8], 1), 0, NODE_DEV - 1).astype(jnp.int32)
    return dict(jac_blocks=jac_blocks, psi_start=psi_start, source=source, pseudo_step=pseudo_step, dissipation=dissipation, freq_volume=freq_volume, normals=normals, face_owner=face_owner, face_slot=face_slot)


def rotate(rim, turn):
    cosine = math.cos(turn)
    sine = math.sin(turn)
    real_part = rim[:, :5]
    imag_part = rim[:, 5:]
    return jnp.concatenate([real_part * cosine - imag_part * sine, real_part * sine + imag_part * cosine], axis=1)


def transpose_apply(tiles, diff):
    total_real = jnp.zeros_like(diff[:, :5])
    total_imag = jnp.zeros_like(diff[:, :5])
    for row_index in range(5):
        column = tiles[:, row_index * 5:row_index * 5 + 5].astype(jnp.float32)
        total_real = total_real + column * diff[:, row_index:row_index + 1]
        total_imag = total_imag + column * diff[:, 5 + row_index:6 + row_index]
    return jnp.concatenate([total_real, total_imag], axis=1)


def reference(jac_blocks, psi_start, source, pseudo_step, dissipation, freq_volume, normals, face_owner, face_slot):
    passes = psi_start.shape[0]
    phase_angle = 2.0 * math.pi * ND * passes / BLADES
    tiles = jac_blocks.reshape(passes, 25, NI, NJ, NK)
    cycle_index = jnp.arange(passes).reshape(passes, 1, 1, 1, 1)
    state = psi_start
    for sweep in range(SWEEPS):
        below_rim = jnp.roll(state[:, :, :, -1:], 1, axis=0)
        below_rim = jnp.where(cycle_index == 0, rotate(below_rim, -phase_angle), below_rim)
        above_rim = jnp.roll(state[:, :, :, :1], -1, axis=0)
        above_rim = jnp.where(cycle_index == passes - 1, rotate(above_rim, phase_angle), above_rim)
        padded_j = jnp.concatenate([below_rim, state, above_rim], axis=3)
        padded_i = jnp.pad(state, ((0, 0), (0, 0), (1, 1), (0, 0), (0, 0)))
        padded_k = jnp.pad(state, ((0, 0), (0, 0), (0, 0), (0, 0), (1, 1)))
        beside = padded_i[:, :, 2:] + padded_i[:, :, :-2]
        beside = beside + padded_j[:, :, :, 2:] + padded_j[:, :, :, :-2]
        beside = beside + padded_k[..., 2:] + padded_k[..., :-2]
        diff = 0.5 * (padded_i[:, :, 2:] - padded_i[:, :, :-2])
        convect = transpose_apply(tiles, diff)
        omega = freq_volume[:, None]
        spin = jnp.concatenate([omega * state[:, 5:], -omega * state[:, :5]], axis=1)
        resid = convect + spin + dissipation[:, None] * (6.0 * state - beside) - source
        state = state - pseudo_step[:, None] * resid
    wall_state = state[..., 0]
    values = jnp.concatenate([normals * wall_state[:, 1:4], normals * wall_state[:, 6:9]], axis=1)
    values = values.reshape(passes, 6, NI * NJ)
    node_ids = (face_owner[..., 0] * NODE_DEV + face_slot).astype(jnp.int32)
    results = []
    for part_index in range(passes):
        summed = jnp.zeros((6, NODES), jnp.float32).at[:, node_ids[part_index]].add(values[part_index])
        results.append(summed)
    return state, jnp.stack(results, axis=0)
```

```python
import functools
import math

import jax
import jax.numpy as jnp
from jax import lax
from jax.experimental import pallas as pl
from jax.experimental.pallas import tpu as pltpu
from jax.sharding import PartitionSpec as P

NODE_DEV = 256
SWEEPS = 2
ND = 1
BLADES = 36
LANES = 128
SUB = 8
CODE = 32767.0
BOUND = 6.0
MESH = pl.DeviceIdType.MESH


def kernel(
    B, passes, phase_angle,
    jac_h, psi_h, source_h, pstep_h, diss_h, freq_h, normals_h, owner_h, slot_h,
    adj, sens,
    jac, source, pstep, diss, freq, normals_v, owner, slot, normals, ids,
    jpack, jsend, jrecv, jflat, pad0, pad1, low, high,
    code0, low0, high0, code1, low1, high1, scale1, low_scale, high_scale,
    rim_send, rim_recv, idbuf, valbuf, hits, turned, wall_send, low_wall, high_wall, rim_wall,
    l_s, j_s, j_r, h_s, h_r, c_s, c_r, w_s, w_r, r_s, r_r, i_s, i_r, v_s, v_r,
):
    me = lax.axis_index("brick")
    mp = lax.axis_index("passage")
    NJ, NK = source.shape[1], source.shape[2]
    R = jac.shape[2] // LANES
    planes = jac.shape[1]
    rows = 25 * R
    pitch = jpack.shape[0] // planes
    others = range(1, B)
    up_p = lax.rem(mp + 1, passes)
    down_p = lax.rem(mp + passes - 1, passes)

    barrier = pltpu.get_barrier_semaphore()
    for d in others:
        pl.semaphore_signal(
            barrier, inc=1, device_id={"brick": lax.rem(me + d, B)}, device_id_type=MESH
        )
    pl.semaphore_signal(barrier, inc=1, device_id={"passage": up_p}, device_id_type=MESH)
    greeted = B
    if passes > 2:
        pl.semaphore_signal(barrier, inc=1, device_id={"passage": down_p}, device_id_type=MESH)
        greeted += 1

    psi = pad0.at[:, pl.ds(SUB, NJ), :]
    loads = [
        pltpu.make_async_copy(src, dst, l_s.at[k])
        for k, (src, dst) in enumerate((
            (jac_h, jac), (psi_h, psi), (owner_h, owner), (slot_h, slot), (normals_h, normals_v),
            (source_h, source), (pstep_h, pstep), (diss_h, diss), (freq_h, freq),
        ))
    ]
    for load in loads:
        load.start()

    @pl.when(me == 0)
    def _():
        low0[...] = jnp.zeros_like(low0)
        low1[...] = jnp.zeros_like(low1)
        low_scale[...] = jnp.zeros_like(low_scale)
        low_wall[...] = jnp.zeros_like(low_wall)

    @pl.when(me == B - 1)
    def _():
        high0[...] = jnp.zeros_like(high0)
        high1[...] = jnp.zeros_like(high1)
        high_scale[...] = jnp.zeros_like(high_scale)
        high_wall[...] = jnp.zeros_like(high_wall)

    loads[0].wait()
    for n in range(25):
        for r in range(R):
            for g in range(planes // SUB):
                x = jac[n, pl.ds(g * SUB, SUB), pl.ds(r * LANES, LANES)].astype(jnp.float32)
                jpack[pl.ds(g * SUB * pitch + r * 25 + n, SUB, stride=pitch), :] = x
    for p in range(planes):
        jsend[p, :, :] = jpack[pl.ds(p * pitch, rows), :].astype(jnp.bfloat16)

    def fill_rims(sweep, field, first, last):
        for c in range(10):
            rim_send[sweep, 0, pl.ds(c, 1), :] = field[c, pl.ds(last, 1), :]
            rim_send[sweep, 1, pl.ds(c, 1), :] = field[c, pl.ds(first, 1), :]

    def rim_copies(sweep):
        return [
            pltpu.make_async_remote_copy(
                src_ref=rim_send.at[sweep, k],
                dst_ref=rim_recv.at[sweep, k],
                send_sem=r_s.at[sweep, k],
                recv_sem=r_r.at[sweep, k],
                device_id={"passage": peer},
                device_id_type=MESH,
            )
            for k, peer in ((0, up_p), (1, down_p))
        ]

    def halo_copies(h_s, h_r, sweep, src, low, high):
        up = pltpu.make_async_remote_copy(
            src_ref=src, dst_ref=low, send_sem=h_s.at[sweep, 0], recv_sem=h_r.at[sweep, 0],
            device_id={"brick": lax.rem(me + 1, B)}, device_id_type=MESH,
        )
        down = pltpu.make_async_remote_copy(
            src_ref=src, dst_ref=high, send_sem=h_s.at[sweep, 1], recv_sem=h_r.at[sweep, 1],
            device_id={"brick": lax.rem(me + B - 1, B)}, device_id_type=MESH,
        )
        return up, down

    def halo_start(up, down):
        @pl.when(me < B - 1)
        def _():
            up.start()

        @pl.when(me > 0)
        def _():
            down.start()

    def halo_recv(up, down):
        @pl.when(me > 0)
        def _():
            up.wait_recv()

        @pl.when(me < B - 1)
        def _():
            down.wait_recv()

    def halo_sent(up, down):
        @pl.when(me < B - 1)
        def _():
            up.wait_send()

        @pl.when(me > 0)
        def _():
            down.wait_send()

    loads[1].wait()
    fill_rims(0, pad0, SUB, SUB + NJ - 1)
    for c in range(10):
        q = jnp.round(pad0[c, pl.ds(SUB, NJ), :] * (CODE / BOUND))
        code0[c, :, :] = q.astype(jnp.int32).astype(jnp.int16)
    loads[2].wait()
    loads[3].wait()
    faces = owner.shape[1]
    ids[...] = jnp.full((SUB, LANES), -1, jnp.int32)
    ids[0:1, pl.ds(0, faces)] = owner[...] * NODE_DEV + slot[...]
    idbuf[pl.ds(me, 1), :, :] = ids[...].reshape(1, SUB, LANES)

    def await_all(ref, sem):
        whole = ref.at[pl.ds(0, B - 1)]
        pltpu.make_async_copy(whole, whole, sem).wait()

    j_copies, id_copies, val_copies = [], [], []
    for k, d in enumerate(list(range(B // 2, B)) + list(range(1, B // 2))[::-1]):
        peer = me
        for b in range(B.bit_length() - 1):
            if d >> b & 1:
                peer = peer + (1 << b) * (1 - 2 * lax.rem(lax.div(me, 1 << b), 2))
        j_copies.append(pltpu.make_async_remote_copy(
            src_ref=jsend.at[peer], dst_ref=jrecv.at[me], send_sem=j_s, recv_sem=j_r,
            device_id={"brick": peer}, device_id_type=MESH))
        id_copies.append(pltpu.make_async_remote_copy(
            src_ref=ids, dst_ref=idbuf.at[me], send_sem=i_s, recv_sem=i_r,
            device_id={"brick": peer}, device_id_type=MESH))
        val_copies.append(pltpu.make_async_remote_copy(
            src_ref=valbuf.at[me], dst_ref=valbuf.at[me], send_sem=v_s, recv_sem=v_r,
            device_id={"brick": peer}, device_id_type=MESH))
    rims0, rims1 = rim_copies(0), rim_copies(1)
    halo0 = halo_copies(h_s, h_r, 0, code0, low0, high0)
    halo1 = halo_copies(h_s, h_r, 1, code1, low1, high1)
    walls = halo_copies(w_s, w_r, 0, wall_send, low_wall, high_wall)
    scales = halo_copies(c_s, c_r, 0, scale1, low_scale, high_scale)

    pl.semaphore_wait(barrier, greeted)
    for copy in id_copies:
        copy.start()
    for copy in j_copies:
        copy.start()
    for copy in rims0:
        copy.start()
    halo_start(*halo0)

    jrecv[pl.ds(me, 1), :, :] = jsend[pl.ds(me, 1), :, :]
    for load in loads[4:]:
        load.wait()
    normals[...] = jnp.zeros_like(normals)
    for d in range(3):
        for k in (d, 3 + d):
            normals[pl.ds(k, 1), pl.ds(0, faces)] = normals_v[d, :, :]

    lane = lax.broadcasted_iota(jnp.int32, (SUB, NK), 1)

    def place_rims(sweep, pad):
        for k, (edge, turn, row) in enumerate(
            ((0, -phase_angle, SUB - 1), (passes - 1, phase_angle, SUB + NJ))
        ):
            rim = rim_recv[sweep, k, :, :]
            re, im = rim[0:5], rim[5:10]
            at_edge = mp == edge
            cosine = jnp.where(at_edge, math.cos(turn), 1.0).astype(jnp.float32)
            sine = jnp.where(at_edge, math.sin(turn), 0.0).astype(jnp.float32)
            re, im = re * cosine - im * sine, re * sine + im * cosine
            if sweep == SWEEPS - 1:
                rim_wall[k, 0:5, :] = re
                rim_wall[k, SUB : SUB + 5, :] = im
            for c in range(5):
                pad[c, pl.ds(row, 1), :] = re[c : c + 1]
                pad[5 + c, pl.ds(row, 1), :] = im[c : c + 1]

    def advance(pad, low, high, out, shift):
        for t in range(NJ // SUB):
            at = pl.ds(t * SUB, SUB)
            om, ds_, ps = freq[at, :], diss[at, :], pstep[at, :]
            us, lows, highs = [], [], []
            for c in range(10):
                us.append(pad[c, pl.ds(SUB + t * SUB, SUB), :])
                lows.append(low[c, at, :])
                highs.append(high[c, at, :])
            diff = [0.5 * (h - l) for h, l in zip(highs, lows)]
            conv = [None] * 10
            for n in range(5):
                for m in range(5):
                    tile = jflat[pl.ds(t * SUB * 25 + n * 5 + m, SUB, stride=25), :]
                    for part in (0, 5):
                        term = tile * diff[part + n]
                        conv[part + m] = term if conv[part + m] is None else conv[part + m] + term
            for c in range(10):
                u = us[c]
                beside = highs[c] + lows[c]
                beside = beside + pad[c, pl.ds(SUB + t * SUB + 1, SUB), :]
                beside = beside + pad[c, pl.ds(SUB + t * SUB - 1, SUB), :]
                beside = beside + jnp.where(lane == NK - 1, 0.0, pltpu.roll(u, NK - 1, 1))
                beside = beside + jnp.where(lane == 0, 0.0, pltpu.roll(u, 1, 1))
                spin = om * us[c + 5] if c < 5 else -(om * us[c - 5])
                resid = conv[c] + spin + ds_ * (6.0 * u - beside) - source[c, at, :]
                out[c, pl.ds(shift + t * SUB, SUB), :] = u - ps * resid

    lanes = lax.broadcasted_iota(jnp.int32, (NJ, NK), 1)

    def turn_over(slot, pieces):
        packed = jnp.zeros((NJ, NK), jnp.float32)
        for to, column, x in pieces:
            shift = (to - column) % NK
            x = pltpu.roll(x, shift, 1) if shift else x
            packed = jnp.where(lanes == to, x, packed)
        if NJ < LANES:
            packed = jnp.concatenate([packed, jnp.zeros((LANES - NJ, NK), jnp.float32)], axis=0)
        turned[slot, :, :] = packed.T

    turn_over(0, [(0, 0, pstep[...]), (1, 0, diss[...]), (2, 0, freq[...])]
              + [(SUB + c + c // 5 * 3, 0, source[c, :, :]) for c in range(10)])
    await_all(idbuf, i_r)
    node = lax.broadcasted_iota(jnp.int32, (NODE_DEV, LANES), 0) + me * NODE_DEV
    for s in range(B):
        hits[s, :, :] = jnp.where(idbuf[s, 0:1, :] == node, 1.0, 0.0).astype(jnp.bfloat16)

    for copy in rims0:
        copy.wait_recv()
    place_rims(0, pad0)
    halo_recv(*halo0)
    for code, field in ((low0, low), (high0, high)):
        for c in range(10):
            field[c, :, :] = code[c, :, :].astype(jnp.int32).astype(jnp.float32) * (BOUND / CODE)
    await_all(jrecv, j_r)
    for s in range(B):
        jflat[pl.ds(s * rows, rows), :] = jrecv[s, :, :].astype(jnp.float32)

    advance(pad0, low, high, pad1, SUB)
    fill_rims(1, pad1, SUB, SUB + NJ - 1)
    for copy in rims1:
        copy.start()
    turn_over(2, [
        (16 * k + c + c // 5 * 3, k, pad1[c, pl.ds(SUB, NJ), :]) for k in range(2) for c in range(10)
    ])
    wall_send[...] = turned[2, 0:16, :]
    halo_start(*walls)
    for c in range(10):
        x = pad1[c, pl.ds(SUB, NJ), :]
        top = jnp.maximum(jnp.max(jnp.abs(x), axis=0, keepdims=True), 1e-30)
        scale1[pl.ds(c, 1), :] = top * (1.0 / CODE)
        code1[c, :, :] = jnp.round(x * (CODE / top)).astype(jnp.int32).astype(jnp.int16)
    halo_start(*scales)
    halo_start(*halo1)
    for copy in rims1:
        copy.wait_recv()
    place_rims(1, pad1)
    turn_over(1, [
        (SUB * n + m, 0, jflat[pl.ds(n * 5 + m, NJ, stride=25), :])
        for n in range(5) for m in range(5)
    ])
    halo_recv(*walls)
    face = lax.broadcasted_iota(jnp.int32, (5, LANES), 1)
    sides = normals[0:3, :]
    valbuf[pl.ds(me, 1), :, :] = jnp.zeros((1, SUB, LANES), jnp.float32)
    for part in range(2):
        at = pl.ds(SUB * part, 5)
        u, lo, hi = turned[2, at, :], low_wall[at, :], high_wall[at, :]
        diff = 0.5 * (hi - lo)
        conv = turned[1, 0:5, :] * diff[0:1]
        for n in range(1, 5):
            conv = conv + turned[1, pl.ds(SUB * n, 5), :] * diff[n : n + 1]
        below = jnp.where(face == 0, rim_wall[0, at, :][:, 0:1], pltpu.roll(u, 1, 1))
        above = jnp.where(face == NJ - 1, rim_wall[1, at, :][:, 0:1], pltpu.roll(u, LANES - 1, 1))
        beside = hi + lo + above + below + turned[2, pl.ds(16 + SUB * part, 5), :]
        spin = turned[0, 2:3, :] * turned[2, pl.ds(SUB * (1 - part), 5), :]
        spin = -spin if part else spin
        resid = conv + spin + turned[0, 1:2, :] * (6.0 * u - beside)
        resid = resid - turned[0, pl.ds(SUB + SUB * part, 5), :]
        fresh = u - turned[0, 0:1, :] * resid
        valbuf[pl.ds(me, 1), pl.ds(3 * part, 3), :] = (fresh[1:4] * sides)[None]
    for copy in val_copies:
        copy.start()

    halo_recv(*scales)
    halo_recv(*halo1)
    for code, scale, field in ((low1, low_scale, low), (high1, high_scale, high)):
        for c in range(10):
            f = code[c, :, :].astype(jnp.int32).astype(jnp.float32)
            field[c, :, :] = f * scale[pl.ds(c, 1), :]
    advance(pad1, low, high, adj, 0)

    await_all(valbuf, v_r)
    total = jnp.zeros((3 * SUB, NODE_DEV), jnp.float32)
    for s in range(B):
        v = valbuf[s, :, :]
        a = v.astype(jnp.bfloat16).astype(jnp.float32)
        rest = v - a
        b = rest.astype(jnp.bfloat16).astype(jnp.float32)
        parts = jnp.concatenate([a, b, rest - b], axis=0).astype(jnp.bfloat16)
        total = total + lax.dot_general(
            parts, hits[s, :, :], (((1,), (1,)), ((), ())), preferred_element_type=jnp.float32
        )
    summed = total[0:SUB] + total[SUB : 2 * SUB] + total[2 * SUB :]
    sens[...] = summed[0:6].reshape(6, 1, NODE_DEV)

    await_all(jsend, j_s)
    await_all(idbuf, i_s)
    await_all(valbuf, v_s)
    for copy in rims0 + rims1:
        copy.wait_send()
    halo_sent(*halo0)
    halo_sent(*halo1)
    halo_sent(*scales)
    halo_sent(*walls)


def hand_over(adj, sens, adj_out, sens_out, out_s):
    outs = [pltpu.make_async_copy(adj, adj_out, out_s.at[0]), pltpu.make_async_copy(sens, sens_out, out_s.at[1])]
    for copy in outs:
        copy.start()
    for copy in outs:
        copy.wait()


def body(B, passes, jac_blocks, psi_start, source, pseudo_step, dissipation, freq_volume,
         normals, face_owner, face_slot):
    _, _, planes_all, cells = jac_blocks.shape
    NJ, NK = psi_start.shape[3:]
    phase_angle = 2.0 * math.pi * ND * passes / BLADES
    R = cells // LANES
    rows = 25 * R
    pitch = -(-rows // SUB) * SUB
    faces = face_slot.shape[1]
    f32 = jnp.float32
    i16 = jnp.int16
    field, plane = (10, NJ, NK), (NJ, NK)
    hbm = pl.BlockSpec(memory_space=pl.ANY)
    vm = pl.BlockSpec(memory_space=pltpu.VMEM)
    dma = pltpu.SemaphoreType.DMA
    adj, sens = pl.pallas_call(
        functools.partial(kernel, B, passes, phase_angle),
        out_shape=(
            pltpu.VMEM(field, f32),
            pltpu.VMEM((6, 1, NODE_DEV), f32),
        ),
        in_specs=[hbm] * 9,
        out_specs=(vm, vm),
        scratch_shapes=[
            pltpu.VMEM((25, planes_all, cells), jnp.bfloat16),
            pltpu.VMEM(field, f32),
            pltpu.VMEM(plane, f32),
            pltpu.VMEM(plane, f32),
            pltpu.VMEM(plane, f32),
            pltpu.VMEM((3, 1, faces), f32),
            pltpu.VMEM((1, faces), jnp.int32),
            pltpu.VMEM((1, faces), jnp.int32),
            pltpu.VMEM((SUB, LANES), f32),
            pltpu.VMEM((SUB, LANES), jnp.int32),
            pltpu.VMEM((planes_all * pitch, LANES), f32),
            pltpu.VMEM((planes_all, rows, LANES), jnp.bfloat16),
            pltpu.VMEM((planes_all, rows, LANES), jnp.bfloat16),
            pltpu.VMEM((B * rows, LANES), f32),
            pltpu.VMEM((10, NJ + 2 * SUB, NK), f32),
            pltpu.VMEM((10, NJ + 2 * SUB, NK), f32),
            pltpu.VMEM(field, f32),
            pltpu.VMEM(field, f32),
            pltpu.VMEM(field, i16),
            pltpu.VMEM(field, i16),
            pltpu.VMEM(field, i16),
            pltpu.VMEM(field, i16),
            pltpu.VMEM(field, i16),
            pltpu.VMEM(field, i16),
            pltpu.VMEM((2 * SUB, NK), f32),
            pltpu.VMEM((2 * SUB, NK), f32),
            pltpu.VMEM((2 * SUB, NK), f32),
            pltpu.VMEM((2, 2, 2 * SUB, NK), f32),
            pltpu.VMEM((2, 2, 2 * SUB, NK), f32),
            pltpu.VMEM((B, SUB, LANES), jnp.int32),
            pltpu.VMEM((B, SUB, LANES), f32),
            pltpu.VMEM((B, NODE_DEV, LANES), jnp.bfloat16),
            pltpu.VMEM((3, NK, LANES), f32),
            pltpu.VMEM((2 * SUB, LANES), f32),
            pltpu.VMEM((2 * SUB, LANES), f32),
            pltpu.VMEM((2 * SUB, LANES), f32),
            pltpu.VMEM((2, 2 * SUB, LANES), f32),
            dma((9,)),
            dma, dma,
            dma((2, 2)), dma((2, 2)),
            dma((1, 2)), dma((1, 2)),
            dma((1, 2)), dma((1, 2)),
            dma((2, 2)), dma((2, 2)),
            dma, dma,
            dma, dma,
        ],
        compiler_params=pltpu.CompilerParams(collective_id=0, has_side_effects=True),
        name="flutter",
    )(jac_blocks[0], psi_start[0, :, 0], source[0, :, 0], pseudo_step[0, 0], dissipation[0, 0],
      freq_volume[0, 0], normals[0], face_owner[:, :, 0], face_slot)
    adj = pltpu.with_memory_space_constraint(adj, pltpu.VMEM)
    sens = pltpu.with_memory_space_constraint(sens, pltpu.VMEM)
    adj, sens = pl.pallas_call(
        hand_over,
        out_shape=(
            jax.ShapeDtypeStruct(field, f32),
            jax.ShapeDtypeStruct((6, 1, NODE_DEV), f32),
        ),
        in_specs=[vm, vm],
        out_specs=(hbm, hbm),
        scratch_shapes=[
            dma((2,)),
        ],
        name="hand_over",
    )(adj, sens)
    return adj[None, :, None], jnp.transpose(sens, (1, 0, 2))


def solution(mesh):
    placed = (
        P("passage", None, None, "brick"),
        P("passage", None, "brick", None, None),
        P("passage", None, "brick", None, None),
        P("passage", "brick", None, None),
        P("passage", "brick", None, None),
        P("passage", "brick", None, None),
        P("passage", None, "brick", None),
        P("passage", "brick", None),
        P("passage", "brick"),
    )
    return jax.shard_map(
        functools.partial(body, mesh.shape["brick"], mesh.shape["passage"]),
        mesh=mesh,
        in_specs=placed,
        out_specs=(P("passage", None, "brick", None, None), P("passage", None, "brick")),
        check_vma=False,
    )
```

```python
import functools
import math

import jax
import jax.numpy as jnp
from jax import lax
from jax.experimental import pallas as pl
from jax.experimental.pallas import tpu as pltpu
from jax.sharding import PartitionSpec as P

NODE_DEV = 256
SWEEPS = 2
ND = 1
BLADES = 36
LANES = 128
SUB = 8
CODE = 32767.0
BOUND = 6.0
MESH = pl.DeviceIdType.MESH


def flip(index, mask, count):
    other = index
    for b in range(count.bit_length() - 1):
        if mask >> b & 1:
            other = other + (1 << b) * (1 - 2 * lax.rem(lax.div(index, 1 << b), 2))
    return other


def kernel(
    B, passes, phase_angle,
    jac_h, psi_h, source_h, pstep_h, diss_h, freq_h, normals_h, owner_h, slot_h,
    adj, sens,
    jac, source, pstep, diss, freq, normals_v, owner, slot,
    jpack, jsend, jrecv, jflat, pad0, pad1,
    code0, low0, high0, code1, low1, high1, rim_send, rim_recv,
    mix, turned, stage, jturn, jwall, jw_send, jw_recv,
    wall, wall_low, wall_high, wall_rim, idbuf, valbuf, hits,
    l_s, j_s, j_r, jw_s, jw_r, i_s, i_r, v_s, v_r,
    h_s, h_r, g_s, g_r, w_s, w_r, r_s, r_r, q_s, q_r,
):
    me = lax.axis_index("brick")
    mp = lax.axis_index("passage")
    NJ, NK = source.shape[1], source.shape[2]
    R = jac.shape[2] // LANES
    planes = jac.shape[1]
    rows = 25 * R
    pitch = jpack.shape[0] // planes
    T = NJ // SUB
    G = SUB // R
    mine = lax.div(me, G)
    up_p = lax.rem(mp + 1, passes)
    down_p = lax.rem(mp + passes - 1, passes)
    f32 = jnp.float32

    barrier = pltpu.get_barrier_semaphore()
    for d in range(1, B):
        pl.semaphore_signal(
            barrier, inc=1, device_id={"brick": lax.rem(me + d, B)}, device_id_type=MESH
        )
    pl.semaphore_signal(barrier, inc=1, device_id={"passage": up_p}, device_id_type=MESH)
    greeted = B
    if passes > 2:
        pl.semaphore_signal(barrier, inc=1, device_id={"passage": down_p}, device_id_type=MESH)
        greeted += 1

    psi = pad0.at[:, pl.ds(SUB, NJ), :]
    loads = [
        pltpu.make_async_copy(src, dst, l_s.at[k])
        for k, (src, dst) in enumerate((
            (psi_h, psi), (jac_h, jac), (owner_h, owner), (slot_h, slot), (normals_h, normals_v),
            (source_h, source), (pstep_h, pstep), (diss_h, diss), (freq_h, freq),
        ))
    ]
    for load in loads:
        load.start()

    @pl.when(me == 0)
    def _():
        low0[...] = jnp.zeros_like(low0)
        low1[...] = jnp.zeros_like(low1)
        wall_low[...] = jnp.zeros_like(wall_low)

    @pl.when(me == B - 1)
    def _():
        high0[...] = jnp.zeros_like(high0)
        high1[...] = jnp.zeros_like(high1)
        wall_high[...] = jnp.zeros_like(wall_high)

    def copy_to(src, dst, send, recv, axis, peer):
        return pltpu.make_async_remote_copy(
            src_ref=src, dst_ref=dst, send_sem=send, recv_sem=recv,
            device_id={axis: peer}, device_id_type=MESH,
        )

    def beside_copies(src, low, high, send, recv):
        up = copy_to(src, low, send.at[0], recv[0], "brick", lax.rem(me + 1, B))
        down = copy_to(src, high, send.at[1], recv[1], "brick", lax.rem(me + B - 1, B))
        return up, down

    def beside_start(up, down):
        @pl.when(me < B - 1)
        def _():
            up.start()

        @pl.when(me > 0)
        def _():
            down.start()

    def beside_recv(up, down):
        @pl.when(me > 0)
        def _():
            up.wait_recv()

        @pl.when(me < B - 1)
        def _():
            down.wait_recv()

    def await_bytes(ref, sem):
        pltpu.make_async_copy(ref, ref, sem).wait()

    def beside_sent(ref, send):
        @pl.when(me < B - 1)
        def _():
            await_bytes(ref, send.at[0])

        @pl.when(me > 0)
        def _():
            await_bytes(ref, send.at[1])

    lanes = lax.broadcasted_iota(jnp.int32, (NJ, NK), 1)
    lane = lax.broadcasted_iota(jnp.int32, (1, LANES), 1)
    sub = lax.broadcasted_iota(jnp.int32, (SUB, NK), 0)
    lane8 = lax.broadcasted_iota(jnp.int32, (SUB, NK), 1)

    def turn_over(slot, pieces):
        halves = [jnp.zeros((NJ, NK), f32), jnp.zeros((NJ, NK), f32)]
        for to, columns, load in pieces:
            x = jnp.concatenate([load(r) for r in range(R)], axis=0) if R > 1 else load(0)
            for half, column in enumerate(columns):
                if column is not None:
                    shift = (to - column) % NK
                    y = pltpu.roll(x, shift, 1) if shift else x
                    halves[half] = jnp.where(lanes == to, y, halves[half])
        turned[slot, :, :] = jnp.concatenate(halves, axis=0).T

    def plane_rows(ref):
        return lambda r: ref[pl.ds(r, B, stride=R), :]

    def field_rows(ref, c, shift):
        return lambda r: ref[c, pl.ds(shift + r, B, stride=R), :]

    def spread(c):
        return c + c // 5 * 3

    loads[0].wait()
    for k, row in enumerate((SUB + NJ - 1, SUB)):
        for c in range(10):
            rim_send[0, k, pl.ds(c, 1), :] = pad0[c, pl.ds(row, 1), :]
    turn_over(
        0,
        [(spread(c), (0, 1), field_rows(pad0, c, SUB)) for c in range(10)]
        + [(2 * SUB + spread(c), (None, 2), field_rows(pad0, c, SUB)) for c in range(10)],
    )
    wall[0, :, :] = turned[0, 0 : 2 * SUB, :]
    for t in range(T):
        for c in range(0, 10, 2):
            at = pl.ds(SUB + t * SUB, SUB)
            x = jnp.concatenate([pad0[c, at, :], pad0[c + 1, at, :]], axis=0)
            q = jnp.round(x * (CODE / BOUND))
            code0[t, pl.ds(c * SUB, 2 * SUB), :] = q.astype(jnp.int32).astype(jnp.int16)

    for k in (2, 3, 4):
        loads[k].wait()
    faces = owner.shape[1]
    mix[...] = jnp.zeros_like(mix)
    mix[0:1, pl.ds(0, faces)] = (owner[...] * NODE_DEV + slot[...]).astype(f32)
    for d in range(3):
        mix[1 + d : 2 + d, pl.ds(0, faces)] = normals_v[d, :, :]
    stage[...] = jnp.concatenate(
        [mix[...], jnp.zeros((LANES - SUB, LANES), f32)], axis=0
    ).T
    x = [stage[pl.ds(r, B, stride=R), :] for r in range(R)]
    mix[...] = jnp.concatenate(x + x, axis=0).T[0:SUB]
    idbuf[pl.ds(me, 1), :, :] = mix[0:1, :].reshape(1, 1, LANES)

    loads[1].wait()
    for n in range(25):
        for r in range(R):
            for g in range(planes // SUB):
                x = jac[n, pl.ds(g * SUB, SUB), pl.ds(r * LANES, LANES)].astype(f32)
                jpack[pl.ds(g * SUB * pitch + r * 25 + n, SUB, stride=pitch), :] = x
    first = lax.broadcasted_iota(jnp.int32, (SUB, LANES), 0) == lane
    first = jnp.where(first, 1.0, 0.0).astype(jnp.bfloat16)
    for p in range(planes):
        x = jpack[pl.ds(p * pitch, pitch), :]
        jsend[p, :, :] = x[0:rows].astype(jnp.bfloat16)
        x = jnp.concatenate([x, jnp.zeros((LANES - pitch, LANES), f32)], axis=0)
        y = lax.dot_general(
            first, x.astype(jnp.bfloat16), (((1,), (1,)), ((), ())), preferred_element_type=f32
        )
        jw_send[p, :, :] = y[0:2]

    j_copies, jw_copies, id_copies, val_copies = [], [], [], []
    for d in list(range(B // 2, B)) + list(range(1, B // 2))[::-1]:
        peer = flip(me, d, B)
        j_copies.append(
            copy_to(jsend.at[peer], jrecv.at[me], j_s, j_r.at[mine], "brick", peer)
        )
        jw_copies.append(copy_to(jw_send.at[peer], jw_recv.at[me], jw_s, jw_r, "brick", peer))
        id_copies.append(copy_to(idbuf.at[me], idbuf.at[me], i_s, i_r, "brick", peer))
        val_copies.append(copy_to(valbuf.at[me], valbuf.at[me], v_s, v_r, "brick", peer))

    def rim_copies(sweep):
        return [
            copy_to(
                rim_send.at[sweep, k], rim_recv.at[sweep, k], r_s.at[k], r_r.at[sweep, k],
                "passage", peer,
            )
            for k, peer in ((0, up_p), (1, down_p))
        ]

    def wall_rims(sweep):
        return [
            copy_to(
                wall.at[sweep], wall_rim.at[sweep, k], q_s.at[k], q_r.at[sweep, k],
                "passage", peer,
            )
            for k, peer in ((0, up_p), (1, down_p))
        ]

    def wall_copies(sweep):
        return beside_copies(
            wall.at[sweep], wall_low.at[sweep], wall_high.at[sweep], w_s,
            (w_r.at[sweep, 0], w_r.at[sweep, 1]),
        )

    def tile_copies(t):
        return beside_copies(
            code1.at[t], low1.at[t], high1.at[t], g_s, (g_r.at[0, t], g_r.at[1, t])
        )

    rims0, rims1 = rim_copies(0), rim_copies(1)
    halo0 = beside_copies(code0, low0, high0, h_s, (h_r.at[0], h_r.at[1]))

    pl.semaphore_wait(barrier, greeted)
    for copy in wall_rims(0) + rims0:
        copy.start()
    beside_start(*wall_copies(0))
    for copy in jw_copies:
        copy.start()
    beside_start(*halo0)
    for copy in j_copies:
        copy.start()
    for copy in id_copies:
        copy.start()

    jrecv[pl.ds(me, 1), :, :] = jsend[pl.ds(me, 1), :, :]
    jw_recv[pl.ds(me, 1), :, :] = jw_send[pl.ds(me, 1), :, :]
    for load in loads[5:]:
        load.wait()
    turn_over(
        1,
        [(k, (0, 1), plane_rows(ref)) for k, ref in enumerate((pstep, diss, freq))]
        + [(SUB + spread(c), (0, 1), field_rows(source, c, 0)) for c in range(10)],
    )

    def rotated(re, im, edge, turn):
        at_edge = mp == edge
        cosine = jnp.where(at_edge, math.cos(turn), 1.0).astype(f32)
        sine = jnp.where(at_edge, math.sin(turn), 0.0).astype(f32)
        return re * cosine - im * sine, re * sine + im * cosine

    def place_rim(sweep, pad, k):
        edge, turn, row = ((0, -phase_angle, SUB - 1), (passes - 1, phase_angle, SUB + NJ))[k]
        rim = rim_recv[sweep, k, :, :]
        parts = rotated(rim[0:5], rim[5:10], edge, turn)
        for c in range(10):
            pad[c, pl.ds(row, 1), :] = parts[c // 5][c % 5 : c % 5 + 1]

    def tile_step(t, pad, low, high, sweep):
        at = pl.ds(pl.multiple_of(t * SUB, SUB), SUB)
        here = pl.ds(pl.multiple_of(t * SUB + SUB, SUB), SUB)
        after = pl.ds(pl.multiple_of(t * SUB + 2 * SUB, SUB), SUB)
        om, ds_, ps = freq[at, :], diss[at, :], pstep[at, :]
        us = [pad[c, here, :] for c in range(10)]
        sides = []
        for ref in (low, high):
            if sweep == 0:
                scale = BOUND / CODE
            else:
                scale = ref[t, pl.ds(10 * SUB, 2 * SUB), :].astype(jnp.int32).astype(f32)[0:SUB]
                scale = scale * (1.0 / (256.0 * CODE))
            side = []
            for c in range(0, 10, 2):
                x = ref[t, pl.ds(c * SUB, 2 * SUB), :].astype(jnp.int32).astype(f32)
                side += [x[0:SUB] * scale, x[SUB : 2 * SUB] * scale]
            sides.append(side)
        lows, highs = sides
        diff = [0.5 * (h - l) for h, l in zip(highs, lows)]
        conv = [None] * 10
        for n in range(5):
            for m in range(5):
                tile = jflat[t, pl.ds(n * 5 + m, SUB, stride=25), :]
                for part in (0, 5):
                    term = tile * diff[part + n]
                    conv[part + m] = term if conv[part + m] is None else conv[part + m] + term
        fresh = []
        for c in range(10):
            u = us[c]
            above = jnp.where(
                sub == SUB - 1, pltpu.roll(pad[c, after, :], SUB - 1, 0), pltpu.roll(u, SUB - 1, 0)
            )
            below = jnp.where(sub == 0, pltpu.roll(pad[c, at, :], 1, 0), pltpu.roll(u, 1, 0))
            beside = highs[c] + lows[c] + above + below
            beside = beside + jnp.where(lane8 == NK - 1, 0.0, pltpu.roll(u, NK - 1, 1))
            beside = beside + jnp.where(lane8 == 0, 0.0, pltpu.roll(u, 1, 1))
            spin = om * us[c + 5] if c < 5 else -(om * us[c - 5])
            resid = conv[c] + spin + ds_ * (6.0 * u - beside) - source[c, at, :]
            fresh.append(u - ps * resid)
        return fresh

    def first_step(u):
        t = flip(mine, u, T)
        @pl.when(t == 0)
        def _():
            rims0[0].wait_recv()
            place_rim(0, pad0, 0)

        @pl.when(t == T - 1)
        def _():
            rims0[1].wait_recv()
            place_rim(0, pad0, 1)

        count = G if u else G - 1
        if count:
            await_bytes(jrecv.at[pl.ds(0, count)], j_r.at[t])
        for g in range(G):
            jflat[t, pl.ds(g * rows, rows), :] = jrecv[t * G + g, :, :].astype(f32)
        fresh = tile_step(t, pad0, low0, high0, 0)
        here = pl.ds(pl.multiple_of(t * SUB + SUB, SUB), SUB)
        top = jnp.abs(fresh[0])
        for c in range(10):
            pad1[c, here, :] = fresh[c]
            top = jnp.maximum(top, jnp.abs(fresh[c]))
        for k, (tile, row) in enumerate(((T - 1, SUB - 1), (0, 0))):
            @pl.when(t == tile)
            def _():
                for c in range(10):
                    rim_send[1, k, pl.ds(c, 1), :] = fresh[c][row : row + 1]
                rims1[k].start()

        top = jnp.floor(jnp.max(top, axis=0, keepdims=True) * 256.0) + 1.0
        top = jnp.broadcast_to(top, (2 * SUB, NK))
        scale = (256.0 * CODE) / top
        for c in range(0, 10, 2):
            x = jnp.concatenate([fresh[c], fresh[c + 1]], axis=0)
            q = jnp.round(x * scale)
            code1[t, pl.ds(c * SUB, 2 * SUB), :] = q.astype(jnp.int32).astype(jnp.int16)
        code1[t, pl.ds(10 * SUB, 2 * SUB), :] = top.astype(jnp.int32).astype(jnp.int16)
        beside_start(*tile_copies(t))

    def second_step(t):
        @pl.when(t == 0)
        def _():
            rims1[0].wait_recv()
            place_rim(1, pad1, 0)

        @pl.when(t == T - 1)
        def _():
            rims1[1].wait_recv()
            place_rim(1, pad1, 1)

        beside_recv(*tile_copies(t))
        fresh = tile_step(t, pad1, low1, high1, 1)
        for c in range(10):
            adj[c, pl.ds(pl.multiple_of(t * SUB, SUB), SUB), :] = fresh[c]

    place = lax.rem(lane, NJ)
    turn_of = lax.div(place, B)

    def wall_step(sweep):
        u16, low16, high16 = wall[sweep, :, :], wall_low[sweep, :, :], wall_high[sweep, :, :]
        fold = (R - 1) * B - 1

        def moved(x, shift):
            shift = shift % LANES
            return pltpu.roll(x, shift, 1) if shift else x

        rims = []
        for k, (edge, turn, shift) in enumerate((
            (0, -phase_angle, 1 - NJ), (passes - 1, phase_angle, NJ - 1),
        )):
            rim = moved(wall_rim[sweep, k, :, :], shift)
            rims.append(rotated(rim[0:5], rim[SUB : SUB + 5], edge, turn))
        out = []
        for part in range(2):
            at = slice(SUB * part, SUB * part + 5)
            other = slice(SUB * (1 - part), SUB * (1 - part) + 5)
            u, lo, hi = u16[at], low16[at], high16[at]
            diff = 0.5 * (hi - lo)
            conv = jwall[0:5, :] * diff[0:1]
            for n in range(1, 5):
                conv = conv + jwall[pl.ds(5 * n, 5), :] * diff[n : n + 1]
            below = jnp.where(turn_of == 0, moved(u, -fold), moved(u, B))
            below = jnp.where(place == 0, rims[0][part], below)
            above = jnp.where(turn_of == R - 1, moved(u, fold), moved(u, -B))
            above = jnp.where(place == NJ - 1, rims[1][part], above)
            beside = hi + lo + above + below + moved(u, NJ)
            if sweep == 0:
                second = turned[0, pl.ds(2 * SUB + SUB * part, 5), :]
                beside = beside + jnp.where(lane < NJ, 0.0, second)
            spin = turned[1, 2:3, :] * u16[other]
            spin = -spin if part else spin
            resid = conv + spin + turned[1, 1:2, :] * (6.0 * u - beside)
            resid = resid - turned[1, pl.ds(SUB + SUB * part, 5), :]
            out.append(u - turned[1, 0:1, :] * resid)
        return out

    def wall_first():
        beside_recv(*wall_copies(0))
        for copy in wall_rims(0):
            copy.wait_recv()
        await_bytes(jw_recv.at[pl.ds(0, B - 1)], jw_r)
        for s in range(B):
            for k in range(2):
                stage[pl.ds(k * B + s, 1), :] = jw_recv[s, pl.ds(k, 1), :]
        jturn[...] = stage[...].T
        total = jnp.zeros((32, LANES), f32)
        for k in range(2):
            for r in range(R):
                x = jturn[pl.ds(r * 25, 32), :]
                shift = k * (NJ - B) + r * B
                x = pltpu.roll(x, shift, 1) if shift else x
                start = k * NJ + r * B
                total = jnp.where((lane >= start) & (lane < start + B), x, total)
        jwall[...] = total
        wall[1, :, :] = jnp.zeros((2 * SUB, LANES), f32)
        for part, fresh in enumerate(wall_step(0)):
            wall[1, pl.ds(SUB * part, 5), :] = fresh
        for copy in wall_rims(1):
            copy.start()
        beside_start(*wall_copies(1))

    def wall_second():
        beside_recv(*wall_copies(1))
        for copy in wall_rims(1):
            copy.wait_recv()
        sides = mix[1:4, :]
        real, imag = [fresh[1:4] * sides for fresh in wall_step(1)]
        both = jnp.where(lane < NJ, real, pltpu.roll(imag, NJ, 1))
        valbuf[pl.ds(me, 1), :, :] = both[None]
        for copy in val_copies:
            copy.start()

    def gather_hits():
        await_bytes(idbuf.at[pl.ds(0, B - 1)], i_r)
        node = lax.broadcasted_iota(jnp.int32, (NODE_DEV, LANES), 0) + me * NODE_DEV
        node = node.astype(f32)
        for s in range(B):
            hits[s, :, :] = jnp.where(idbuf[s, :, :] == node, 1.0, 0.0).astype(jnp.bfloat16)

    def sum_nodes():
        await_bytes(valbuf.at[pl.ds(0, B - 1)], v_r)
        total = jnp.zeros((3 * SUB, NODE_DEV), f32)
        for s in range(B):
            v = valbuf[s, :, :]
            v = jnp.concatenate(
                [jnp.where(lane < NJ, v, 0.0), jnp.where(lane < NJ, 0.0, v), jnp.zeros((2, LANES), f32)],
                axis=0,
            )
            a = v.astype(jnp.bfloat16).astype(f32)
            rest = v - a
            b = rest.astype(jnp.bfloat16).astype(f32)
            parts = jnp.concatenate([a, b, rest - b], axis=0).astype(jnp.bfloat16)
            total = total + lax.dot_general(
                parts, hits[s, :, :], (((1,), (1,)), ((), ())), preferred_element_type=f32
            )
        summed = total[0:SUB] + total[SUB : 2 * SUB] + total[2 * SUB :]
        sens[...] = summed[0:6].reshape(6, 1, NODE_DEV)

    half = T // 2
    upper = lax.div(mine, half)

    def second_order(i):
        near = half - 1 - i + upper * (1 + 2 * i)
        far = half + i - upper * (1 + 2 * i)
        return near, far

    wall_first()
    beside_recv(*halo0)
    for u in range(half):
        first_step(u)
    first_step(half)
    wall_second()
    for u in range(half + 1, T):
        first_step(u)
    for side in range(2):
        for i in range(half - 1):
            second_step(second_order(i)[side])
    gather_hits()
    sum_nodes()
    for side in range(2):
        second_step(second_order(half - 1)[side])
    await_bytes(jsend.at[pl.ds(0, B - 1)], j_s)
    await_bytes(jw_send.at[pl.ds(0, B - 1)], jw_s)
    await_bytes(idbuf.at[pl.ds(0, B - 1)], i_s)
    await_bytes(valbuf.at[pl.ds(0, B - 1)], v_s)
    for k in range(2):
        await_bytes(rim_send.at[k], r_s.at[k])
        await_bytes(wall, q_s.at[k])
    beside_sent(code0, h_s)
    beside_sent(code1, g_s)
    beside_sent(wall, w_s)


def hand_over(adj, sens, adj_out, sens_out, out_s):
    outs = [pltpu.make_async_copy(adj, adj_out, out_s.at[0]), pltpu.make_async_copy(sens, sens_out, out_s.at[1])]
    for copy in outs:
        copy.start()
    for copy in outs:
        copy.wait()


def body(B, passes, jac_blocks, psi_start, source, pseudo_step, dissipation, freq_volume,
         normals, face_owner, face_slot):
    _, _, planes_all, cells = jac_blocks.shape
    NJ, NK = psi_start.shape[3:]
    phase_angle = 2.0 * math.pi * ND * passes / BLADES
    R = cells // LANES
    rows = 25 * R
    pitch = -(-rows // SUB) * SUB
    faces = face_slot.shape[1]
    T = NJ // SUB
    f32 = jnp.float32
    i16 = jnp.int16
    bf16 = jnp.bfloat16
    field, plane = (10, NJ, NK), (NJ, NK)
    coded, scaled = (T, 10 * SUB, NK), (T, 12 * SUB, NK)
    hbm = pl.BlockSpec(memory_space=pl.ANY)
    vm = pl.BlockSpec(memory_space=pltpu.VMEM)
    dma = pltpu.SemaphoreType.DMA
    adj, sens = pl.pallas_call(
        functools.partial(kernel, B, passes, phase_angle),
        out_shape=(
            pltpu.VMEM(field, f32),
            pltpu.VMEM((6, 1, NODE_DEV), f32),
        ),
        in_specs=[hbm] * 9,
        out_specs=(vm, vm),
        scratch_shapes=[
            pltpu.VMEM((25, planes_all, cells), bf16),
            pltpu.VMEM(field, f32),
            pltpu.VMEM(plane, f32),
            pltpu.VMEM(plane, f32),
            pltpu.VMEM(plane, f32),
            pltpu.VMEM((3, 1, faces), f32),
            pltpu.VMEM((1, faces), jnp.int32),
            pltpu.VMEM((1, faces), jnp.int32),
            pltpu.VMEM((planes_all * pitch, LANES), f32),
            pltpu.VMEM((planes_all, rows, LANES), bf16),
            pltpu.VMEM((planes_all, rows, LANES), bf16),
            pltpu.VMEM((T, 25 * SUB, LANES), f32),
            pltpu.VMEM((10, NJ + 2 * SUB, NK), f32),
            pltpu.VMEM((10, NJ + 2 * SUB, NK), f32),
            pltpu.VMEM(coded, i16),
            pltpu.VMEM(coded, i16),
            pltpu.VMEM(coded, i16),
            pltpu.VMEM(scaled, i16),
            pltpu.VMEM(scaled, i16),
            pltpu.VMEM(scaled, i16),
            pltpu.VMEM((2, 2, 2 * SUB, NK), f32),
            pltpu.VMEM((2, 2, 2 * SUB, NK), f32),
            pltpu.VMEM((SUB, LANES), f32),
            pltpu.VMEM((2, LANES, LANES), f32),
            pltpu.VMEM((LANES, LANES), f32),
            pltpu.VMEM((LANES, LANES), f32),
            pltpu.VMEM((32, LANES), f32),
            pltpu.VMEM((planes_all, 2, LANES), f32),
            pltpu.VMEM((planes_all, 2, LANES), f32),
            pltpu.VMEM((2, 2 * SUB, LANES), f32),
            pltpu.VMEM((2, 2 * SUB, LANES), f32),
            pltpu.VMEM((2, 2 * SUB, LANES), f32),
            pltpu.VMEM((2, 2, 2 * SUB, LANES), f32),
            pltpu.VMEM((B, 1, LANES), f32),
            pltpu.VMEM((B, 3, LANES), f32),
            pltpu.VMEM((B, NODE_DEV, LANES), bf16),
            dma((9,)),
            dma, dma((T,)),
            dma, dma,
            dma, dma,
            dma, dma,
            dma((2,)), dma((2,)),
            dma((2,)), dma((2, T)),
            dma((2,)), dma((2, 2)),
            dma((2,)), dma((2, 2)),
            dma((2,)), dma((2, 2)),
        ],
        compiler_params=pltpu.CompilerParams(collective_id=0, has_side_effects=True),
        name="flutter",
    )(jac_blocks[0], psi_start[0, :, 0], source[0, :, 0], pseudo_step[0, 0], dissipation[0, 0],
      freq_volume[0, 0], normals[0], face_owner[:, :, 0], face_slot)
    adj = pltpu.with_memory_space_constraint(adj, pltpu.VMEM)
    sens = pltpu.with_memory_space_constraint(sens, pltpu.VMEM)
    adj, sens = pl.pallas_call(
        hand_over,
        out_shape=(
            jax.ShapeDtypeStruct(field, f32),
            jax.ShapeDtypeStruct((6, 1, NODE_DEV), f32),
        ),
        in_specs=[vm, vm],
        out_specs=(hbm, hbm),
        scratch_shapes=[
            dma((2,)),
        ],
        name="hand_over",
    )(adj, sens)
    return adj[None, :, None], jnp.transpose(sens, (1, 0, 2))


def solution(mesh):
    placed = (
        P("passage", None, None, "brick"),
        P("passage", None, "brick", None, None),
        P("passage", None, "brick", None, None),
        P("passage", "brick", None, None),
        P("passage", "brick", None, None),
        P("passage", "brick", None, None),
        P("passage", None, "brick", None),
        P("passage", "brick", None),
        P("passage", "brick"),
    )
    return jax.shard_map(
        functools.partial(body, mesh.shape["brick"], mesh.shape["passage"]),
        mesh=mesh,
        in_specs=placed,
        out_specs=(P("passage", None, "brick", None, None), P("passage", None, "brick")),
        check_vma=False,
    )
```

```python
import functools
import math

import jax
import jax.numpy as jnp
from jax import lax
from jax.experimental import pallas as pl
from jax.experimental.pallas import tpu as pltpu
from jax.sharding import PartitionSpec as P

NODE_DEV = 256
SWEEPS = 2
ND = 1
BLADES = 36
LANES = 128
SUB = 8
CODE = 32767.0
BOUND = 6.0
MESH = pl.DeviceIdType.MESH


def flip(index, mask, count):
    other = index
    for b in range(count.bit_length() - 1):
        if mask >> b & 1:
            other = other + (1 << b) * (1 - 2 * lax.rem(lax.div(index, 1 << b), 2))
    return other


def kernel(
    B, passes, phase_angle,
    jac_h, psi_h, source_h, pstep_h, diss_h, freq_h, normals_h, owner_h, slot_h,
    adj, sens,
    jac, source, pstep, diss, freq, normals_v, owner, slot,
    jpack, jsend, jrecv, jflat, pad0, pad1,
    code0, low0, high0, code1, low1, high1, rim_send, rim_recv,
    mix, turned, stage, jturn, jwall, jw_send, jw_recv,
    wall, wall_low, wall_high, wall_rim, idbuf, valbuf, hits,
    l_s, j_s, j_r, jw_s, jw_r, i_s, i_r, v_s, v_r,
    h_s, h_r, g_s, g_r, w_s, w_r, r_s, r_r, q_s, q_r,
):
    me = lax.axis_index("brick")
    mp = lax.axis_index("passage")
    NJ, NK = source.shape[1], source.shape[2]
    R = jac.shape[2] // LANES
    planes = jac.shape[1]
    rows = 25 * R
    pitch = jpack.shape[0] // planes
    T = NJ // SUB
    G = SUB // R
    mine = lax.div(me, G)
    up_p = lax.rem(mp + 1, passes)
    down_p = lax.rem(mp + passes - 1, passes)
    f32 = jnp.float32

    barrier = pltpu.get_barrier_semaphore()
    for d in range(1, B):
        pl.semaphore_signal(
            barrier, inc=1, device_id={"brick": lax.rem(me + d, B)}, device_id_type=MESH
        )
    pl.semaphore_signal(barrier, inc=1, device_id={"passage": up_p}, device_id_type=MESH)
    greeted = B
    if passes > 2:
        pl.semaphore_signal(barrier, inc=1, device_id={"passage": down_p}, device_id_type=MESH)
        greeted += 1

    psi = pad0.at[:, pl.ds(SUB, NJ), :]
    loads = [
        pltpu.make_async_copy(src, dst, l_s.at[k])
        for k, (src, dst) in enumerate((
            (psi_h, psi), (jac_h, jac), (owner_h, owner), (slot_h, slot), (normals_h, normals_v),
            (source_h, source), (pstep_h, pstep), (diss_h, diss), (freq_h, freq),
        ))
    ]
    for load in loads:
        load.start()

    @pl.when(me == 0)
    def _():
        low0[...] = jnp.zeros_like(low0)
        low1[...] = jnp.zeros_like(low1)
        wall_low[...] = jnp.zeros_like(wall_low)

    @pl.when(me == B - 1)
    def _():
        high0[...] = jnp.zeros_like(high0)
        high1[...] = jnp.zeros_like(high1)
        wall_high[...] = jnp.zeros_like(wall_high)

    def copy_to(src, dst, send, recv, axis, peer):
        return pltpu.make_async_remote_copy(
            src_ref=src, dst_ref=dst, send_sem=send, recv_sem=recv,
            device_id={axis: peer}, device_id_type=MESH,
        )

    def beside_copies(src, low, high, send, recv):
        up = copy_to(src, low, send.at[0], recv[0], "brick", lax.rem(me + 1, B))
        down = copy_to(src, high, send.at[1], recv[1], "brick", lax.rem(me + B - 1, B))
        return up, down

    def beside_start(up, down):
        @pl.when(me < B - 1)
        def _():
            up.start()

        @pl.when(me > 0)
        def _():
            down.start()

    def beside_recv(up, down):
        @pl.when(me > 0)
        def _():
            up.wait_recv()

        @pl.when(me < B - 1)
        def _():
            down.wait_recv()

    def await_bytes(ref, sem):
        pltpu.make_async_copy(ref, ref, sem).wait()

    def beside_sent(ref, send):
        @pl.when(me < B - 1)
        def _():
            await_bytes(ref, send.at[0])

        @pl.when(me > 0)
        def _():
            await_bytes(ref, send.at[1])

    lanes = lax.broadcasted_iota(jnp.int32, (NJ, NK), 1)
    lane = lax.broadcasted_iota(jnp.int32, (1, LANES), 1)
    sub = lax.broadcasted_iota(jnp.int32, (SUB, NK), 0)
    lane8 = lax.broadcasted_iota(jnp.int32, (SUB, NK), 1)

    def turn_over(slot, pieces):
        halves = [jnp.zeros((NJ, NK), f32), jnp.zeros((NJ, NK), f32)]
        for to, columns, load in pieces:
            x = jnp.concatenate([load(r) for r in range(R)], axis=0) if R > 1 else load(0)
            for half, column in enumerate(columns):
                if column is not None:
                    shift = (to - column) % NK
                    y = pltpu.roll(x, shift, 1) if shift else x
                    halves[half] = jnp.where(lanes == to, y, halves[half])
        turned[slot, :, :] = jnp.concatenate(halves, axis=0).T

    def plane_rows(ref):
        return lambda r: ref[pl.ds(r, B, stride=R), :]

    def field_rows(ref, c, shift):
        return lambda r: ref[c, pl.ds(shift + r, B, stride=R), :]

    def spread(c):
        return c + c // 5 * 3

    loads[0].wait()
    for k, row in enumerate((SUB + NJ - 1, SUB)):
        for c in range(10):
            rim_send[0, k, pl.ds(c, 1), :] = pad0[c, pl.ds(row, 1), :]
    turn_over(
        0,
        [(spread(c), (0, 1), field_rows(pad0, c, SUB)) for c in range(10)]
        + [(2 * SUB + spread(c), (None, 2), field_rows(pad0, c, SUB)) for c in range(10)],
    )
    wall[0, :, :] = turned[0, 0 : 2 * SUB, :]
    for t in range(T):
        for c in range(0, 10, 2):
            at = pl.ds(SUB + t * SUB, SUB)
            x = jnp.concatenate([pad0[c, at, :], pad0[c + 1, at, :]], axis=0)
            q = jnp.round(x * (CODE / BOUND))
            code0[t, pl.ds(c * SUB, 2 * SUB), :] = q.astype(jnp.int32).astype(jnp.int16)

    loads[1].wait()
    for n in range(25):
        for r in range(R):
            for g in range(planes // SUB):
                x = jac[n, pl.ds(g * SUB, SUB), pl.ds(r * LANES, LANES)].astype(f32)
                jpack[pl.ds(g * SUB * pitch + r * 25 + n, SUB, stride=pitch), :] = x
    first = lax.broadcasted_iota(jnp.int32, (SUB, LANES), 0) == lane
    first = jnp.where(first, 1.0, 0.0).astype(jnp.bfloat16)
    for p in range(planes):
        x = jpack[pl.ds(p * pitch, pitch), :]
        jsend[p, :, :] = x[0:rows].astype(jnp.bfloat16)
        x = jnp.concatenate([x, jnp.zeros((LANES - pitch, LANES), f32)], axis=0)
        y = lax.dot_general(
            first, x.astype(jnp.bfloat16), (((1,), (1,)), ((), ())), preferred_element_type=f32
        )
        jw_send[p, :, :] = y[0:2]

    j_copies, jw_copies, id_copies, val_copies = [], [], [], []
    for d in list(range(B // 2, B)) + list(range(1, B // 2))[::-1]:
        peer = flip(me, d, B)
        j_copies.append(
            copy_to(jsend.at[peer], jrecv.at[me], j_s, j_r.at[mine], "brick", peer)
        )
        jw_copies.append(copy_to(jw_send.at[peer], jw_recv.at[me], jw_s, jw_r, "brick", peer))
        id_copies.append(copy_to(idbuf.at[me], idbuf.at[me], i_s, i_r, "brick", peer))
        val_copies.append(copy_to(valbuf.at[me], valbuf.at[me], v_s, v_r, "brick", peer))

    def rim_copies(sweep):
        return [
            copy_to(
                rim_send.at[sweep, k], rim_recv.at[sweep, k], r_s.at[k], r_r.at[sweep, k],
                "passage", peer,
            )
            for k, peer in ((0, up_p), (1, down_p))
        ]

    def wall_rims(sweep):
        return [
            copy_to(
                wall.at[sweep], wall_rim.at[sweep, k], q_s.at[k], q_r.at[sweep, k],
                "passage", peer,
            )
            for k, peer in ((0, up_p), (1, down_p))
        ]

    def wall_copies(sweep):
        return beside_copies(
            wall.at[sweep], wall_low.at[sweep], wall_high.at[sweep], w_s,
            (w_r.at[sweep, 0], w_r.at[sweep, 1]),
        )

    def tile_copies(t):
        return beside_copies(
            code1.at[t], low1.at[t], high1.at[t], g_s, (g_r.at[0, t], g_r.at[1, t])
        )

    rims0, rims1 = rim_copies(0), rim_copies(1)
    half = T // 2
    upper = lax.div(mine, half)

    def side_of(brick):
        return lax.div(lax.div(brick, G), half)

    def halo_copies(k):
        copies = []
        for step, dst in ((1, low0), (B - 1, high0)):
            peer = lax.rem(me + step, B)
            side = side_of(peer)
            part = side if k == 0 else 1 - side
            at = pl.ds(part * half, half)
            copies.append(copy_to(
                code0.at[at], dst.at[at], h_s.at[0 if step == 1 else 1],
                h_r.at[0 if step == 1 else 1, k], "brick", peer,
            ))
        return copies

    def halo_recv(k):
        part = upper if k == 0 else 1 - upper
        at = pl.ds(part * half, half)

        @pl.when(me > 0)
        def _():
            await_bytes(low0.at[at], h_r.at[0, k])

        @pl.when(me < B - 1)
        def _():
            await_bytes(high0.at[at], h_r.at[1, k])

    pl.semaphore_wait(barrier, greeted)
    for copy in wall_rims(0) + rims0:
        copy.start()
    beside_start(*wall_copies(0))
    for copy in jw_copies:
        copy.start()
    beside_start(*halo_copies(0))
    for copy in j_copies[:B // 4]:
        copy.start()
    beside_start(*halo_copies(1))
    for copy in j_copies[B // 2 :]:
        copy.start()

    jrecv[pl.ds(me, 1), :, :] = jsend[pl.ds(me, 1), :, :]
    jw_recv[pl.ds(me, 1), :, :] = jw_send[pl.ds(me, 1), :, :]
    for load in loads[5:]:
        load.wait()
    turn_over(
        1,
        [(k, (0, 1), plane_rows(ref)) for k, ref in enumerate((pstep, diss, freq))]
        + [(SUB + spread(c), (0, 1), field_rows(source, c, 0)) for c in range(10)],
    )

    for k in (2, 3, 4):
        loads[k].wait()
    faces = owner.shape[1]
    mix[...] = jnp.zeros_like(mix)
    mix[0:1, pl.ds(0, faces)] = (owner[...] * NODE_DEV + slot[...]).astype(f32)
    for d in range(3):
        mix[1 + d : 2 + d, pl.ds(0, faces)] = normals_v[d, :, :]
    stage[...] = jnp.concatenate(
        [mix[...], jnp.zeros((LANES - SUB, LANES), f32)], axis=0
    ).T
    x = [stage[pl.ds(r, B, stride=R), :] for r in range(R)]
    mix[...] = jnp.concatenate(x + x, axis=0).T[0:SUB]
    idbuf[pl.ds(me, 1), :, :] = mix[0:1, :].reshape(1, 1, LANES)
    for copy in id_copies:
        copy.start()

    def rotated(re, im, edge, turn):
        at_edge = mp == edge
        cosine = jnp.where(at_edge, math.cos(turn), 1.0).astype(f32)
        sine = jnp.where(at_edge, math.sin(turn), 0.0).astype(f32)
        return re * cosine - im * sine, re * sine + im * cosine

    def place_rim(sweep, pad, k):
        edge, turn, row = ((0, -phase_angle, SUB - 1), (passes - 1, phase_angle, SUB + NJ))[k]
        rim = rim_recv[sweep, k, :, :]
        parts = rotated(rim[0:5], rim[5:10], edge, turn)
        for c in range(10):
            pad[c, pl.ds(row, 1), :] = parts[c // 5][c % 5 : c % 5 + 1]

    def tile_step(t, pad, low, high, sweep):
        at = pl.ds(pl.multiple_of(t * SUB, SUB), SUB)
        here = pl.ds(pl.multiple_of(t * SUB + SUB, SUB), SUB)
        after = pl.ds(pl.multiple_of(t * SUB + 2 * SUB, SUB), SUB)
        om, ds_, ps = freq[at, :], diss[at, :], pstep[at, :]
        us = [pad[c, here, :] for c in range(10)]
        sides = []
        for ref in (low, high):
            if sweep == 0:
                scale = BOUND / CODE
            else:
                scale = ref[t, pl.ds(10 * SUB, 2 * SUB), :].astype(jnp.int32).astype(f32)[0:SUB]
                scale = scale * (1.0 / (256.0 * CODE))
            side = []
            for c in range(0, 10, 2):
                x = ref[t, pl.ds(c * SUB, 2 * SUB), :].astype(jnp.int32).astype(f32)
                side += [x[0:SUB] * scale, x[SUB : 2 * SUB] * scale]
            sides.append(side)
        lows, highs = sides
        diff = [0.5 * (h - l) for h, l in zip(highs, lows)]
        conv = [None] * 10
        for n in range(5):
            for m in range(5):
                tile = jflat[t, pl.ds(n * 5 + m, SUB, stride=25), :]
                for part in (0, 5):
                    term = tile * diff[part + n]
                    conv[part + m] = term if conv[part + m] is None else conv[part + m] + term
        fresh = []
        for c in range(10):
            u = us[c]
            above = jnp.where(
                sub == SUB - 1, pltpu.roll(pad[c, after, :], SUB - 1, 0), pltpu.roll(u, SUB - 1, 0)
            )
            below = jnp.where(sub == 0, pltpu.roll(pad[c, at, :], 1, 0), pltpu.roll(u, 1, 0))
            beside = highs[c] + lows[c] + above + below
            beside = beside + jnp.where(lane8 == NK - 1, 0.0, pltpu.roll(u, NK - 1, 1))
            beside = beside + jnp.where(lane8 == 0, 0.0, pltpu.roll(u, 1, 1))
            spin = om * us[c + 5] if c < 5 else -(om * us[c - 5])
            resid = conv[c] + spin + ds_ * (6.0 * u - beside) - source[c, at, :]
            fresh.append(u - ps * resid)
        return fresh

    def first_step(u):
        t = flip(mine, u, T)
        @pl.when(t == 0)
        def _():
            rims0[0].wait_recv()
            place_rim(0, pad0, 0)

        @pl.when(t == T - 1)
        def _():
            rims0[1].wait_recv()
            place_rim(0, pad0, 1)

        count = G if u else G - 1
        if count:
            await_bytes(jrecv.at[pl.ds(0, count)], j_r.at[t])
        for g in range(G):
            jflat[t, pl.ds(g * rows, rows), :] = jrecv[t * G + g, :, :].astype(f32)
        fresh = tile_step(t, pad0, low0, high0, 0)
        here = pl.ds(pl.multiple_of(t * SUB + SUB, SUB), SUB)
        top = jnp.abs(fresh[0])
        for c in range(10):
            pad1[c, here, :] = fresh[c]
            top = jnp.maximum(top, jnp.abs(fresh[c]))
        for k, (tile, row) in enumerate(((T - 1, SUB - 1), (0, 0))):
            @pl.when(t == tile)
            def _():
                for c in range(10):
                    rim_send[1, k, pl.ds(c, 1), :] = fresh[c][row : row + 1]
                rims1[k].start()

        top = jnp.floor(jnp.max(top, axis=0, keepdims=True) * 256.0) + 1.0
        top = jnp.broadcast_to(top, (2 * SUB, NK))
        scale = (256.0 * CODE) / top
        for c in range(0, 10, 2):
            x = jnp.concatenate([fresh[c], fresh[c + 1]], axis=0)
            q = jnp.round(x * scale)
            code1[t, pl.ds(c * SUB, 2 * SUB), :] = q.astype(jnp.int32).astype(jnp.int16)
        code1[t, pl.ds(10 * SUB, 2 * SUB), :] = top.astype(jnp.int32).astype(jnp.int16)
        beside_start(*tile_copies(t))

    def second_step(t):
        @pl.when(t == 0)
        def _():
            rims1[0].wait_recv()
            place_rim(1, pad1, 0)

        @pl.when(t == T - 1)
        def _():
            rims1[1].wait_recv()
            place_rim(1, pad1, 1)

        beside_recv(*tile_copies(t))
        fresh = tile_step(t, pad1, low1, high1, 1)
        for c in range(10):
            adj[c, pl.ds(pl.multiple_of(t * SUB, SUB), SUB), :] = fresh[c]

    place = lax.rem(lane, NJ)
    turn_of = lax.div(place, B)

    def wall_step(sweep):
        u16, low16, high16 = wall[sweep, :, :], wall_low[sweep, :, :], wall_high[sweep, :, :]
        fold = (R - 1) * B - 1

        def moved(x, shift):
            shift = shift % LANES
            return pltpu.roll(x, shift, 1) if shift else x

        rims = []
        for k, (edge, turn, shift) in enumerate((
            (0, -phase_angle, 1 - NJ), (passes - 1, phase_angle, NJ - 1),
        )):
            rim = moved(wall_rim[sweep, k, :, :], shift)
            rims.append(rotated(rim[0:5], rim[SUB : SUB + 5], edge, turn))
        out = []
        for part in range(2):
            at = slice(SUB * part, SUB * part + 5)
            other = slice(SUB * (1 - part), SUB * (1 - part) + 5)
            u, lo, hi = u16[at], low16[at], high16[at]
            diff = 0.5 * (hi - lo)
            conv = jwall[0:5, :] * diff[0:1]
            for n in range(1, 5):
                conv = conv + jwall[pl.ds(5 * n, 5), :] * diff[n : n + 1]
            below = jnp.where(turn_of == 0, moved(u, -fold), moved(u, B))
            below = jnp.where(place == 0, rims[0][part], below)
            above = jnp.where(turn_of == R - 1, moved(u, fold), moved(u, -B))
            above = jnp.where(place == NJ - 1, rims[1][part], above)
            beside = hi + lo + above + below + moved(u, NJ)
            if sweep == 0:
                second = turned[0, pl.ds(2 * SUB + SUB * part, 5), :]
                beside = beside + jnp.where(lane < NJ, 0.0, second)
            spin = turned[1, 2:3, :] * u16[other]
            spin = -spin if part else spin
            resid = conv + spin + turned[1, 1:2, :] * (6.0 * u - beside)
            resid = resid - turned[1, pl.ds(SUB + SUB * part, 5), :]
            out.append(u - turned[1, 0:1, :] * resid)
        return out

    def wall_first():
        beside_recv(*wall_copies(0))
        for copy in wall_rims(0):
            copy.wait_recv()
        await_bytes(jw_recv.at[pl.ds(0, B - 1)], jw_r)
        for s in range(B):
            for k in range(2):
                stage[pl.ds(k * B + s, 1), :] = jw_recv[s, pl.ds(k, 1), :]
        jturn[...] = stage[...].T
        total = jnp.zeros((32, LANES), f32)
        for k in range(2):
            for r in range(R):
                x = jturn[pl.ds(r * 25, 32), :]
                shift = k * (NJ - B) + r * B
                x = pltpu.roll(x, shift, 1) if shift else x
                start = k * NJ + r * B
                total = jnp.where((lane >= start) & (lane < start + B), x, total)
        jwall[...] = total
        wall[1, :, :] = jnp.zeros((2 * SUB, LANES), f32)
        for part, fresh in enumerate(wall_step(0)):
            wall[1, pl.ds(SUB * part, 5), :] = fresh
        for copy in wall_rims(1):
            copy.start()
        beside_start(*wall_copies(1))

    def wall_second():
        beside_recv(*wall_copies(1))
        for copy in wall_rims(1):
            copy.wait_recv()
        sides = mix[1:4, :]
        real, imag = [fresh[1:4] * sides for fresh in wall_step(1)]
        both = jnp.where(lane < NJ, real, pltpu.roll(imag, NJ, 1))
        valbuf[pl.ds(me, 1), :, :] = both[None]
        for copy in val_copies:
            copy.start()

    def gather_hits():
        await_bytes(idbuf.at[pl.ds(0, B - 1)], i_r)
        node = lax.broadcasted_iota(jnp.int32, (NODE_DEV, LANES), 0) + me * NODE_DEV
        node = node.astype(f32)
        for s in range(B):
            hits[s, :, :] = jnp.where(idbuf[s, :, :] == node, 1.0, 0.0).astype(jnp.bfloat16)

    def sum_nodes():
        await_bytes(valbuf.at[pl.ds(0, B - 1)], v_r)
        total = jnp.zeros((3 * SUB, NODE_DEV), f32)
        for s in range(B):
            v = valbuf[s, :, :]
            v = jnp.concatenate(
                [jnp.where(lane < NJ, v, 0.0), jnp.where(lane < NJ, 0.0, v), jnp.zeros((2, LANES), f32)],
                axis=0,
            )
            a = v.astype(jnp.bfloat16).astype(f32)
            rest = v - a
            b = rest.astype(jnp.bfloat16).astype(f32)
            parts = jnp.concatenate([a, b, rest - b], axis=0).astype(jnp.bfloat16)
            total = total + lax.dot_general(
                parts, hits[s, :, :], (((1,), (1,)), ((), ())), preferred_element_type=f32
            )
        summed = total[0:SUB] + total[SUB : 2 * SUB] + total[2 * SUB :]
        sens[...] = summed[0:6].reshape(6, 1, NODE_DEV)

    spot = lax.rem(mine, half)

    def differ(p, q):
        out = 0
        for b in range(half.bit_length() - 1):
            one = lax.rem(lax.div(p, 1 << b) + lax.div(q, 1 << b), 2)
            out = out + (1 << b) * one
        return out

    def near_tile(i):
        return half - 1 - i + upper * (1 + 2 * i)

    def far_tile(i):
        outer = (1 - upper) * (half - 1)
        turn = differ(spot, outer)
        if i < half - 1:
            turn = i + lax.div(i + half - turn, half)
        return (1 - upper) * half + differ(spot, turn)

    wall_first()
    for copy in j_copies[B // 4 : B // 2]:
        copy.start()
    halo_recv(0)
    for u in range(half):
        first_step(u)
    wall_second()
    halo_recv(1)
    first_step(half)
    for u in range(half + 1, T):
        first_step(u)
    for i in range(half - 1):
        second_step(near_tile(i))
    gather_hits()
    for i in range(half - 1):
        second_step(far_tile(i))
    second_step(near_tile(half - 1))
    second_step(far_tile(half - 1))
    sum_nodes()
    await_bytes(jsend.at[pl.ds(0, B - 1)], j_s)
    await_bytes(jw_send.at[pl.ds(0, B - 1)], jw_s)
    await_bytes(idbuf.at[pl.ds(0, B - 1)], i_s)
    await_bytes(valbuf.at[pl.ds(0, B - 1)], v_s)
    for k in range(2):
        await_bytes(rim_send.at[k], r_s.at[k])
        await_bytes(wall, q_s.at[k])
    beside_sent(code0, h_s)
    beside_sent(code1, g_s)
    beside_sent(wall, w_s)


def hand_over(adj, sens, adj_out, sens_out, out_s):
    outs = [pltpu.make_async_copy(adj, adj_out, out_s.at[0]), pltpu.make_async_copy(sens, sens_out, out_s.at[1])]
    for copy in outs:
        copy.start()
    for copy in outs:
        copy.wait()


def body(B, passes, jac_blocks, psi_start, source, pseudo_step, dissipation, freq_volume,
         normals, face_owner, face_slot):
    _, _, planes_all, cells = jac_blocks.shape
    NJ, NK = psi_start.shape[3:]
    phase_angle = 2.0 * math.pi * ND * passes / BLADES
    R = cells // LANES
    rows = 25 * R
    pitch = -(-rows // SUB) * SUB
    faces = face_slot.shape[1]
    T = NJ // SUB
    f32 = jnp.float32
    i16 = jnp.int16
    bf16 = jnp.bfloat16
    field, plane = (10, NJ, NK), (NJ, NK)
    coded, scaled = (T, 10 * SUB, NK), (T, 12 * SUB, NK)
    hbm = pl.BlockSpec(memory_space=pl.ANY)
    vm = pl.BlockSpec(memory_space=pltpu.VMEM)
    dma = pltpu.SemaphoreType.DMA
    adj, sens = pl.pallas_call(
        functools.partial(kernel, B, passes, phase_angle),
        out_shape=(
            pltpu.VMEM(field, f32),
            pltpu.VMEM((6, 1, NODE_DEV), f32),
        ),
        in_specs=[hbm] * 9,
        out_specs=(vm, vm),
        scratch_shapes=[
            pltpu.VMEM((25, planes_all, cells), bf16),
            pltpu.VMEM(field, f32),
            pltpu.VMEM(plane, f32),
            pltpu.VMEM(plane, f32),
            pltpu.VMEM(plane, f32),
            pltpu.VMEM((3, 1, faces), f32),
            pltpu.VMEM((1, faces), jnp.int32),
            pltpu.VMEM((1, faces), jnp.int32),
            pltpu.VMEM((planes_all * pitch, LANES), f32),
            pltpu.VMEM((planes_all, rows, LANES), bf16),
            pltpu.VMEM((planes_all, rows, LANES), bf16),
            pltpu.VMEM((T, 25 * SUB, LANES), f32),
            pltpu.VMEM((10, NJ + 2 * SUB, NK), f32),
            pltpu.VMEM((10, NJ + 2 * SUB, NK), f32),
            pltpu.VMEM(coded, i16),
            pltpu.VMEM(coded, i16),
            pltpu.VMEM(coded, i16),
            pltpu.VMEM(scaled, i16),
            pltpu.VMEM(scaled, i16),
            pltpu.VMEM(scaled, i16),
            pltpu.VMEM((2, 2, 2 * SUB, NK), f32),
            pltpu.VMEM((2, 2, 2 * SUB, NK), f32),
            pltpu.VMEM((SUB, LANES), f32),
            pltpu.VMEM((2, LANES, LANES), f32),
            pltpu.VMEM((LANES, LANES), f32),
            pltpu.VMEM((LANES, LANES), f32),
            pltpu.VMEM((32, LANES), f32),
            pltpu.VMEM((planes_all, 2, LANES), f32),
            pltpu.VMEM((planes_all, 2, LANES), f32),
            pltpu.VMEM((2, 2 * SUB, LANES), f32),
            pltpu.VMEM((2, 2 * SUB, LANES), f32),
            pltpu.VMEM((2, 2 * SUB, LANES), f32),
            pltpu.VMEM((2, 2, 2 * SUB, LANES), f32),
            pltpu.VMEM((B, 1, LANES), f32),
            pltpu.VMEM((B, 3, LANES), f32),
            pltpu.VMEM((B, NODE_DEV, LANES), bf16),
            dma((9,)),
            dma, dma((T,)),
            dma, dma,
            dma, dma,
            dma, dma,
            dma((2,)), dma((2, 2)),
            dma((2,)), dma((2, T)),
            dma((2,)), dma((2, 2)),
            dma((2,)), dma((2, 2)),
            dma((2,)), dma((2, 2)),
        ],
        compiler_params=pltpu.CompilerParams(collective_id=0, has_side_effects=True),
        name="flutter",
    )(jac_blocks[0], psi_start[0, :, 0], source[0, :, 0], pseudo_step[0, 0], dissipation[0, 0],
      freq_volume[0, 0], normals[0], face_owner[:, :, 0], face_slot)
    adj = pltpu.with_memory_space_constraint(adj, pltpu.VMEM)
    sens = pltpu.with_memory_space_constraint(sens, pltpu.VMEM)
    adj, sens = pl.pallas_call(
        hand_over,
        out_shape=(
            jax.ShapeDtypeStruct(field, f32),
            jax.ShapeDtypeStruct((6, 1, NODE_DEV), f32),
        ),
        in_specs=[vm, vm],
        out_specs=(hbm, hbm),
        scratch_shapes=[
            dma((2,)),
        ],
        name="hand_over",
    )(adj, sens)
    return adj[None, :, None], jnp.transpose(sens, (1, 0, 2))


def solution(mesh):
    placed = (
        P("passage", None, None, "brick"),
        P("passage", None, "brick", None, None),
        P("passage", None, "brick", None, None),
        P("passage", "brick", None, None),
        P("passage", "brick", None, None),
        P("passage", "brick", None, None),
        P("passage", None, "brick", None),
        P("passage", "brick", None),
        P("passage", "brick"),
    )
    return jax.shard_map(
        functools.partial(body, mesh.shape["brick"], mesh.shape["passage"]),
        mesh=mesh,
        in_specs=placed,
        out_specs=(P("passage", None, "brick", None, None), P("passage", None, "brick")),
        check_vma=False,
    )
```

```python
import functools
import math

import jax
import jax.numpy as jnp
from jax import lax
from jax.experimental import pallas as pl
from jax.experimental.pallas import tpu as pltpu
from jax.sharding import PartitionSpec as P

NODE_DEV = 256
SWEEPS = 2
ND = 1
BLADES = 36
LANES = 128
SUB = 8
CODE = 32767.0
BOUND = 6.0
MESH = pl.DeviceIdType.MESH


def flip(index, mask, count):
    other = index
    for b in range(count.bit_length() - 1):
        if mask >> b & 1:
            other = other + (1 << b) * (1 - 2 * lax.rem(lax.div(index, 1 << b), 2))
    return other


def kernel(
    B, passes, phase_angle,
    jac_h, psi_h, source_h, pstep_h, diss_h, freq_h, normals_h, owner_h, slot_h,
    adj, sens,
    jac, source, pstep, diss, freq, normals_v, owner, slot,
    jpack, jsend, jrecv, jflat, pad0, pad1,
    code0, low0, high0, code1, low1, high1, rim_send, rim_recv,
    mix, turned, stage, jturn, jwall, jw_send, jw_recv,
    wall, wall_low, wall_high, wall_rim, idbuf, valbuf, hits,
    l_s, j_s, j_r, jw_s, jw_r, i_s, i_r, v_s, v_r,
    h_s, h_r, g_s, g_r, w_s, w_r, r_s, r_r, q_s, q_r,
):
    me = lax.axis_index("brick")
    mp = lax.axis_index("passage")
    NJ, NK = source.shape[1], source.shape[2]
    R = jac.shape[2] // LANES
    planes = jac.shape[1]
    rows = 25 * R
    pitch = jpack.shape[0] // planes
    T = NJ // SUB
    G = SUB // R
    mine = lax.div(me, G)
    up_p = lax.rem(mp + 1, passes)
    down_p = lax.rem(mp + passes - 1, passes)
    f32 = jnp.float32

    barrier = pltpu.get_barrier_semaphore()
    for d in range(1, B):
        pl.semaphore_signal(
            barrier, inc=1, device_id={"brick": lax.rem(me + d, B)}, device_id_type=MESH
        )
    pl.semaphore_signal(barrier, inc=1, device_id={"passage": up_p}, device_id_type=MESH)
    greeted = B
    if passes > 2:
        pl.semaphore_signal(barrier, inc=1, device_id={"passage": down_p}, device_id_type=MESH)
        greeted += 1

    psi = pad0.at[:, pl.ds(SUB, NJ), :]
    loads = [
        pltpu.make_async_copy(src, dst, l_s.at[k])
        for k, (src, dst) in enumerate((
            (psi_h, psi), (jac_h, jac), (owner_h, owner), (slot_h, slot), (normals_h, normals_v),
            (source_h, source), (pstep_h, pstep), (diss_h, diss), (freq_h, freq),
        ))
    ]
    for load in loads:
        load.start()

    @pl.when(me == 0)
    def _():
        low0[...] = jnp.zeros_like(low0)
        low1[...] = jnp.zeros_like(low1)
        wall_low[...] = jnp.zeros_like(wall_low)

    @pl.when(me == B - 1)
    def _():
        high0[...] = jnp.zeros_like(high0)
        high1[...] = jnp.zeros_like(high1)
        wall_high[...] = jnp.zeros_like(wall_high)

    def copy_to(src, dst, send, recv, axis, peer):
        return pltpu.make_async_remote_copy(
            src_ref=src, dst_ref=dst, send_sem=send, recv_sem=recv,
            device_id={axis: peer}, device_id_type=MESH,
        )

    def beside_copies(src, low, high, send, recv):
        up = copy_to(src, low, send.at[0], recv[0], "brick", lax.rem(me + 1, B))
        down = copy_to(src, high, send.at[1], recv[1], "brick", lax.rem(me + B - 1, B))
        return up, down

    def beside_start(up, down):
        @pl.when(me < B - 1)
        def _():
            up.start()

        @pl.when(me > 0)
        def _():
            down.start()

    def beside_recv(up, down):
        @pl.when(me > 0)
        def _():
            up.wait_recv()

        @pl.when(me < B - 1)
        def _():
            down.wait_recv()

    def await_bytes(ref, sem):
        pltpu.make_async_copy(ref, ref, sem).wait()

    def beside_sent(ref, send):
        @pl.when(me < B - 1)
        def _():
            await_bytes(ref, send.at[0])

        @pl.when(me > 0)
        def _():
            await_bytes(ref, send.at[1])

    lanes = lax.broadcasted_iota(jnp.int32, (NJ, NK), 1)
    lane = lax.broadcasted_iota(jnp.int32, (1, LANES), 1)
    sub = lax.broadcasted_iota(jnp.int32, (SUB, NK), 0)
    lane8 = lax.broadcasted_iota(jnp.int32, (SUB, NK), 1)

    def turn_over(slot, pieces):
        halves = [jnp.zeros((NJ, NK), f32), jnp.zeros((NJ, NK), f32)]
        for to, columns, load in pieces:
            x = jnp.concatenate([load(r) for r in range(R)], axis=0) if R > 1 else load(0)
            for half, column in enumerate(columns):
                if column is not None:
                    shift = (to - column) % NK
                    y = pltpu.roll(x, shift, 1) if shift else x
                    halves[half] = jnp.where(lanes == to, y, halves[half])
        turned[slot, :, :] = jnp.concatenate(halves, axis=0).T

    def plane_rows(ref):
        return lambda r: ref[pl.ds(r, B, stride=R), :]

    def field_rows(ref, c, shift):
        return lambda r: ref[c, pl.ds(shift + r, B, stride=R), :]

    def spread(c):
        return c + c // 5 * 3

    loads[0].wait()
    for k, row in enumerate((SUB + NJ - 1, SUB)):
        for c in range(10):
            rim_send[0, k, pl.ds(c, 1), :] = pad0[c, pl.ds(row, 1), :]
    turn_over(
        0,
        [(spread(c), (0, 1), field_rows(pad0, c, SUB)) for c in range(10)]
        + [(2 * SUB + spread(c), (None, 2), field_rows(pad0, c, SUB)) for c in range(10)],
    )
    wall[0, :, :] = turned[0, 0 : 2 * SUB, :]
    for t in range(T):
        for c in range(0, 10, 2):
            at = pl.ds(SUB + t * SUB, SUB)
            x = jnp.concatenate([pad0[c, at, :], pad0[c + 1, at, :]], axis=0)
            q = jnp.round(x * (CODE / BOUND))
            code0[t, pl.ds(c * SUB, 2 * SUB), :] = q.astype(jnp.int32).astype(jnp.int16)

    loads[1].wait()
    for n in range(25):
        for r in range(R):
            for g in range(planes // SUB):
                x = jac[n, pl.ds(g * SUB, SUB), pl.ds(r * LANES, LANES)].astype(f32)
                jpack[pl.ds(g * SUB * pitch + r * 25 + n, SUB, stride=pitch), :] = x
    first = lax.broadcasted_iota(jnp.int32, (SUB, LANES), 0) == lane
    first = jnp.where(first, 1.0, 0.0).astype(jnp.bfloat16)
    for p in range(planes):
        x = jpack[pl.ds(p * pitch, pitch), :]
        jsend[p, :, :] = x[0:rows].astype(jnp.bfloat16)
        x = jnp.concatenate([x, jnp.zeros((LANES - pitch, LANES), f32)], axis=0)
        y = lax.dot_general(
            first, x.astype(jnp.bfloat16), (((1,), (1,)), ((), ())), preferred_element_type=f32
        )
        jw_send[p, :, :] = y[0:2]

    j_copies, jw_copies, id_copies, val_copies = [], [], [], []
    for d in list(range(B // 2, B)) + list(range(1, B // 2))[::-1]:
        peer = flip(me, d, B)
        j_copies.append(
            copy_to(jsend.at[peer], jrecv.at[me], j_s, j_r.at[mine], "brick", peer)
        )
        jw_copies.append(copy_to(jw_send.at[peer], jw_recv.at[me], jw_s, jw_r, "brick", peer))
        id_copies.append(copy_to(idbuf.at[me], idbuf.at[me], i_s, i_r, "brick", peer))
        val_copies.append([
            copy_to(valbuf.at[me], valbuf.at[me], v_s, v_r.at[k], "brick", peer) for k in range(2)
        ])

    centres = (B // 2 - 1, B // 2)
    central = jnp.logical_or(me == centres[0], me == centres[1])

    def rim_copies(sweep):
        return [
            copy_to(
                rim_send.at[sweep, k], rim_recv.at[sweep, k], r_s.at[k], r_r.at[sweep, k],
                "passage", peer,
            )
            for k, peer in ((0, up_p), (1, down_p))
        ]

    def wall_rims(sweep):
        return [
            copy_to(
                wall.at[sweep], wall_rim.at[sweep, k], q_s.at[k], q_r.at[sweep, k],
                "passage", peer,
            )
            for k, peer in ((0, up_p), (1, down_p))
        ]

    def wall_copies(sweep):
        return beside_copies(
            wall.at[sweep], wall_low.at[sweep], wall_high.at[sweep], w_s,
            (w_r.at[sweep, 0], w_r.at[sweep, 1]),
        )

    def tile_copies(t):
        return beside_copies(
            code1.at[t], low1.at[t], high1.at[t], g_s, (g_r.at[0, t], g_r.at[1, t])
        )

    rims0, rims1 = rim_copies(0), rim_copies(1)
    half = T // 2
    upper = lax.div(mine, half)

    def side_of(brick):
        return lax.div(lax.div(brick, G), half)

    def halo_copies(k):
        copies = []
        for step, dst in ((1, low0), (B - 1, high0)):
            peer = lax.rem(me + step, B)
            side = side_of(peer)
            part = side if k == 0 else 1 - side
            at = pl.ds(part * half, half)
            copies.append(copy_to(
                code0.at[at], dst.at[at], h_s.at[0 if step == 1 else 1],
                h_r.at[0 if step == 1 else 1, k], "brick", peer,
            ))
        return copies

    def halo_recv(k):
        part = upper if k == 0 else 1 - upper
        at = pl.ds(part * half, half)

        @pl.when(me > 0)
        def _():
            await_bytes(low0.at[at], h_r.at[0, k])

        @pl.when(me < B - 1)
        def _():
            await_bytes(high0.at[at], h_r.at[1, k])

    pl.semaphore_wait(barrier, greeted)
    for copy in wall_rims(0) + rims0:
        copy.start()
    beside_start(*wall_copies(0))
    for copy in jw_copies:
        copy.start()
    beside_start(*halo_copies(0))
    for copy in j_copies[:B // 4]:
        copy.start()
    beside_start(*halo_copies(1))
    for copy in j_copies[B // 2 :]:
        copy.start()

    jrecv[pl.ds(me, 1), :, :] = jsend[pl.ds(me, 1), :, :]
    jw_recv[pl.ds(me, 1), :, :] = jw_send[pl.ds(me, 1), :, :]
    for load in loads[5:]:
        load.wait()
    turn_over(
        1,
        [(k, (0, 1), plane_rows(ref)) for k, ref in enumerate((pstep, diss, freq))]
        + [(SUB + spread(c), (0, 1), field_rows(source, c, 0)) for c in range(10)],
    )

    for k in (2, 3, 4):
        loads[k].wait()
    faces = owner.shape[1]
    mix[...] = jnp.zeros_like(mix)
    mix[0:1, pl.ds(0, faces)] = (owner[...] * NODE_DEV + slot[...]).astype(f32)
    for d in range(3):
        mix[1 + d : 2 + d, pl.ds(0, faces)] = normals_v[d, :, :]
    stage[...] = jnp.concatenate(
        [mix[...], jnp.zeros((LANES - SUB, LANES), f32)], axis=0
    ).T
    x = [stage[pl.ds(r, B, stride=R), :] for r in range(R)]
    mix[...] = jnp.concatenate(x + x, axis=0).T[0:SUB]
    idbuf[pl.ds(me, 1), :, :] = mix[0:1, :].reshape(1, 1, LANES)
    for copy in id_copies:
        copy.start()

    def rotated(re, im, edge, turn):
        at_edge = mp == edge
        cosine = jnp.where(at_edge, math.cos(turn), 1.0).astype(f32)
        sine = jnp.where(at_edge, math.sin(turn), 0.0).astype(f32)
        return re * cosine - im * sine, re * sine + im * cosine

    def place_rim(sweep, pad, k):
        edge, turn, row = ((0, -phase_angle, SUB - 1), (passes - 1, phase_angle, SUB + NJ))[k]
        rim = rim_recv[sweep, k, :, :]
        parts = rotated(rim[0:5], rim[5:10], edge, turn)
        for c in range(10):
            pad[c, pl.ds(row, 1), :] = parts[c // 5][c % 5 : c % 5 + 1]

    def tile_step(t, pad, low, high, sweep):
        at = pl.ds(pl.multiple_of(t * SUB, SUB), SUB)
        here = pl.ds(pl.multiple_of(t * SUB + SUB, SUB), SUB)
        after = pl.ds(pl.multiple_of(t * SUB + 2 * SUB, SUB), SUB)
        om, ds_, ps = freq[at, :], diss[at, :], pstep[at, :]
        us = [pad[c, here, :] for c in range(10)]
        sides = []
        for ref in (low, high):
            if sweep == 0:
                scale = BOUND / CODE
            else:
                scale = ref[t, pl.ds(10 * SUB, 2), :].astype(jnp.int32).astype(f32)[0:1]
                scale = scale * (1.0 / (256.0 * CODE))
            side = []
            for c in range(0, 10, 2):
                x = ref[t, pl.ds(c * SUB, 2 * SUB), :].astype(jnp.int32).astype(f32)
                side += [x[0:SUB] * scale, x[SUB : 2 * SUB] * scale]
            sides.append(side)
        lows, highs = sides
        diff = [0.5 * (h - l) for h, l in zip(highs, lows)]
        conv = [None] * 10
        for n in range(5):
            for m in range(5):
                tile = jflat[t, pl.ds(n * 5 + m, SUB, stride=25), :]
                for part in (0, 5):
                    term = tile * diff[part + n]
                    conv[part + m] = term if conv[part + m] is None else conv[part + m] + term
        fresh = []
        for c in range(10):
            u = us[c]
            above = jnp.where(
                sub == SUB - 1, pltpu.roll(pad[c, after, :], SUB - 1, 0), pltpu.roll(u, SUB - 1, 0)
            )
            below = jnp.where(sub == 0, pltpu.roll(pad[c, at, :], 1, 0), pltpu.roll(u, 1, 0))
            beside = highs[c] + lows[c] + above + below
            beside = beside + jnp.where(lane8 == NK - 1, 0.0, pltpu.roll(u, NK - 1, 1))
            beside = beside + jnp.where(lane8 == 0, 0.0, pltpu.roll(u, 1, 1))
            spin = om * us[c + 5] if c < 5 else -(om * us[c - 5])
            resid = conv[c] + spin + ds_ * (6.0 * u - beside) - source[c, at, :]
            fresh.append(u - ps * resid)
        return fresh

    def first_step(u):
        t = flip(mine, u, T)
        @pl.when(t == 0)
        def _():
            rims0[0].wait_recv()
            place_rim(0, pad0, 0)

        @pl.when(t == T - 1)
        def _():
            rims0[1].wait_recv()
            place_rim(0, pad0, 1)

        count = G if u else G - 1
        if count:
            await_bytes(jrecv.at[pl.ds(0, count)], j_r.at[t])
        for g in range(G):
            jflat[t, pl.ds(g * rows, rows), :] = jrecv[t * G + g, :, :].astype(f32)
        fresh = tile_step(t, pad0, low0, high0, 0)
        here = pl.ds(pl.multiple_of(t * SUB + SUB, SUB), SUB)
        top = jnp.abs(fresh[0])
        for c in range(10):
            pad1[c, here, :] = fresh[c]
            top = jnp.maximum(top, jnp.abs(fresh[c]))
        for k, (tile, row) in enumerate(((T - 1, SUB - 1), (0, 0))):
            @pl.when(t == tile)
            def _():
                for c in range(10):
                    rim_send[1, k, pl.ds(c, 1), :] = fresh[c][row : row + 1]
                rims1[k].start()

        top = jnp.floor(jnp.max(top, axis=0, keepdims=True) * 256.0) + 1.0
        top = jnp.broadcast_to(top, (2 * SUB, NK))
        scale = (256.0 * CODE) / top
        for c in range(0, 10, 2):
            x = jnp.concatenate([fresh[c], fresh[c + 1]], axis=0)
            q = jnp.round(x * scale)
            code1[t, pl.ds(c * SUB, 2 * SUB), :] = q.astype(jnp.int32).astype(jnp.int16)
        code1[t, pl.ds(10 * SUB, 2), :] = top[0:2].astype(jnp.int32).astype(jnp.int16)
        beside_start(*tile_copies(t))

    def second_step(t):
        @pl.when(t == 0)
        def _():
            rims1[0].wait_recv()
            place_rim(1, pad1, 0)

        @pl.when(t == T - 1)
        def _():
            rims1[1].wait_recv()
            place_rim(1, pad1, 1)

        beside_recv(*tile_copies(t))
        fresh = tile_step(t, pad1, low1, high1, 1)
        for c in range(10):
            adj[c, pl.ds(pl.multiple_of(t * SUB, SUB), SUB), :] = fresh[c]

    place = lax.rem(lane, NJ)
    turn_of = lax.div(place, B)

    def wall_step(sweep):
        u16, low16, high16 = wall[sweep, :, :], wall_low[sweep, :, :], wall_high[sweep, :, :]
        fold = (R - 1) * B - 1

        def moved(x, shift):
            shift = shift % LANES
            return pltpu.roll(x, shift, 1) if shift else x

        rims = []
        for k, (edge, turn, shift) in enumerate((
            (0, -phase_angle, 1 - NJ), (passes - 1, phase_angle, NJ - 1),
        )):
            rim = moved(wall_rim[sweep, k, :, :], shift)
            rims.append(rotated(rim[0:5], rim[SUB : SUB + 5], edge, turn))
        out = []
        for part in range(2):
            at = slice(SUB * part, SUB * part + 5)
            other = slice(SUB * (1 - part), SUB * (1 - part) + 5)
            u, lo, hi = u16[at], low16[at], high16[at]
            diff = 0.5 * (hi - lo)
            conv = jwall[0:5, :] * diff[0:1]
            for n in range(1, 5):
                conv = conv + jwall[pl.ds(5 * n, 5), :] * diff[n : n + 1]
            below = jnp.where(turn_of == 0, moved(u, -fold), moved(u, B))
            below = jnp.where(place == 0, rims[0][part], below)
            above = jnp.where(turn_of == R - 1, moved(u, fold), moved(u, -B))
            above = jnp.where(place == NJ - 1, rims[1][part], above)
            beside = hi + lo + above + below + moved(u, NJ)
            if sweep == 0:
                second = turned[0, pl.ds(2 * SUB + SUB * part, 5), :]
                beside = beside + jnp.where(lane < NJ, 0.0, second)
            spin = turned[1, 2:3, :] * u16[other]
            spin = -spin if part else spin
            resid = conv + spin + turned[1, 1:2, :] * (6.0 * u - beside)
            resid = resid - turned[1, pl.ds(SUB + SUB * part, 5), :]
            out.append(u - turned[1, 0:1, :] * resid)
        return out

    def wall_first():
        beside_recv(*wall_copies(0))
        for copy in wall_rims(0):
            copy.wait_recv()
        await_bytes(jw_recv.at[pl.ds(0, B - 1)], jw_r)
        for s in range(B):
            for k in range(2):
                stage[pl.ds(k * B + s, 1), :] = jw_recv[s, pl.ds(k, 1), :]
        jturn[...] = stage[...].T
        total = jnp.zeros((32, LANES), f32)
        for k in range(2):
            for r in range(R):
                x = jturn[pl.ds(r * 25, 32), :]
                shift = k * (NJ - B) + r * B
                x = pltpu.roll(x, shift, 1) if shift else x
                start = k * NJ + r * B
                total = jnp.where((lane >= start) & (lane < start + B), x, total)
        jwall[...] = total
        wall[1, :, :] = jnp.zeros((2 * SUB, LANES), f32)
        for part, fresh in enumerate(wall_step(0)):
            wall[1, pl.ds(SUB * part, 5), :] = fresh
        for copy in wall_rims(1):
            copy.start()
        beside_start(*wall_copies(1))

    def wall_second():
        beside_recv(*wall_copies(1))
        for copy in wall_rims(1):
            copy.wait_recv()
        sides = mix[1:4, :]
        real, imag = [fresh[1:4] * sides for fresh in wall_step(1)]
        both = jnp.where(lane < NJ, real, pltpu.roll(imag, NJ, 1))
        valbuf[pl.ds(me, 1), :, :] = both[None]

        @pl.when(central)
        def _():
            for copies in val_copies:
                copies[1].start()

        @pl.when(jnp.logical_not(central))
        def _():
            for copies in val_copies:
                copies[0].start()

    def gather_hits():
        await_bytes(idbuf.at[pl.ds(0, B - 1)], i_r)
        node = lax.broadcasted_iota(jnp.int32, (NODE_DEV, LANES), 0) + me * NODE_DEV
        node = node.astype(f32)
        for s in range(B):
            hits[s, :, :] = jnp.where(idbuf[s, :, :] == node, 1.0, 0.0).astype(jnp.bfloat16)

    def sum_nodes(late, total):
        @pl.when(central)
        def _():
            await_bytes(valbuf.at[pl.ds(0, 1 if late else B - 2)], v_r.at[late])

        @pl.when(jnp.logical_not(central))
        def _():
            await_bytes(valbuf.at[pl.ds(0, 2 if late else B - 3)], v_r.at[late])

        for s in centres if late else [s for s in range(B) if s not in centres]:
            v = valbuf[s, :, :]
            v = jnp.concatenate(
                [jnp.where(lane < NJ, v, 0.0), jnp.where(lane < NJ, 0.0, v), jnp.zeros((2, LANES), f32)],
                axis=0,
            )
            a = v.astype(jnp.bfloat16).astype(f32)
            rest = v - a
            b = rest.astype(jnp.bfloat16).astype(f32)
            parts = jnp.concatenate([a, b, rest - b], axis=0).astype(jnp.bfloat16)
            total = total + lax.dot_general(
                parts, hits[s, :, :], (((1,), (1,)), ((), ())), preferred_element_type=f32
            )
        return total

    spot = lax.rem(mine, half)

    def differ(p, q):
        out = 0
        for b in range(half.bit_length() - 1):
            one = lax.rem(lax.div(p, 1 << b) + lax.div(q, 1 << b), 2)
            out = out + (1 << b) * one
        return out

    def near_tile(i):
        return half - 1 - i + upper * (1 + 2 * i)

    def far_tile(i):
        outer = (1 - upper) * (half - 1)
        turn = differ(spot, outer)
        if i < half - 1:
            turn = i + lax.div(i + half - turn, half)
        return (1 - upper) * half + differ(spot, turn)

    wall_first()
    for copy in j_copies[B // 4 : B // 2]:
        copy.start()
    halo_recv(0)
    for u in range(half):
        first_step(u)
    wall_second()
    halo_recv(1)
    first_step(half)
    for u in range(half + 1, T):
        first_step(u)
    gather_hits()
    total = sum_nodes(0, jnp.zeros((3 * SUB, NODE_DEV), f32))
    for i in range(half - 1):
        second_step(near_tile(i))
    for i in range(half - 1):
        second_step(far_tile(i))
    second_step(near_tile(half - 1))
    second_step(far_tile(half - 1))
    total = sum_nodes(1, total)
    summed = total[0:SUB] + total[SUB : 2 * SUB] + total[2 * SUB :]
    sens[...] = summed[0:6].reshape(6, 1, NODE_DEV)
    await_bytes(jsend.at[pl.ds(0, B - 1)], j_s)
    await_bytes(jw_send.at[pl.ds(0, B - 1)], jw_s)
    await_bytes(idbuf.at[pl.ds(0, B - 1)], i_s)
    await_bytes(valbuf.at[pl.ds(0, B - 1)], v_s)
    for k in range(2):
        await_bytes(rim_send.at[k], r_s.at[k])
        await_bytes(wall, q_s.at[k])
    beside_sent(code0, h_s)
    beside_sent(code1, g_s)
    beside_sent(wall, w_s)


def hand_over(adj, sens, adj_out, sens_out, out_s):
    outs = [pltpu.make_async_copy(adj, adj_out, out_s.at[0]), pltpu.make_async_copy(sens, sens_out, out_s.at[1])]
    for copy in outs:
        copy.start()
    for copy in outs:
        copy.wait()


def body(B, passes, jac_blocks, psi_start, source, pseudo_step, dissipation, freq_volume,
         normals, face_owner, face_slot):
    _, _, planes_all, cells = jac_blocks.shape
    NJ, NK = psi_start.shape[3:]
    phase_angle = 2.0 * math.pi * ND * passes / BLADES
    R = cells // LANES
    rows = 25 * R
    pitch = -(-rows // SUB) * SUB
    faces = face_slot.shape[1]
    T = NJ // SUB
    f32 = jnp.float32
    i16 = jnp.int16
    bf16 = jnp.bfloat16
    field, plane = (10, NJ, NK), (NJ, NK)
    coded, scaled = (T, 10 * SUB, NK), (T, 10 * SUB + 2, NK)
    hbm = pl.BlockSpec(memory_space=pl.ANY)
    vm = pl.BlockSpec(memory_space=pltpu.VMEM)
    dma = pltpu.SemaphoreType.DMA
    adj, sens = pl.pallas_call(
        functools.partial(kernel, B, passes, phase_angle),
        out_shape=(
            pltpu.VMEM(field, f32),
            pltpu.VMEM((6, 1, NODE_DEV), f32),
        ),
        in_specs=[hbm] * 9,
        out_specs=(vm, vm),
        scratch_shapes=[
            pltpu.VMEM((25, planes_all, cells), bf16),
            pltpu.VMEM(field, f32),
            pltpu.VMEM(plane, f32),
            pltpu.VMEM(plane, f32),
            pltpu.VMEM(plane, f32),
            pltpu.VMEM((3, 1, faces), f32),
            pltpu.VMEM((1, faces), jnp.int32),
            pltpu.VMEM((1, faces), jnp.int32),
            pltpu.VMEM((planes_all * pitch, LANES), f32),
            pltpu.VMEM((planes_all, rows, LANES), bf16),
            pltpu.VMEM((planes_all, rows, LANES), bf16),
            pltpu.VMEM((T, 25 * SUB, LANES), f32),
            pltpu.VMEM((10, NJ + 2 * SUB, NK), f32),
            pltpu.VMEM((10, NJ + 2 * SUB, NK), f32),
            pltpu.VMEM(coded, i16),
            pltpu.VMEM(coded, i16),
            pltpu.VMEM(coded, i16),
            pltpu.VMEM(scaled, i16),
            pltpu.VMEM(scaled, i16),
            pltpu.VMEM(scaled, i16),
            pltpu.VMEM((2, 2, 2 * SUB, NK), f32),
            pltpu.VMEM((2, 2, 2 * SUB, NK), f32),
            pltpu.VMEM((SUB, LANES), f32),
            pltpu.VMEM((2, LANES, LANES), f32),
            pltpu.VMEM((LANES, LANES), f32),
            pltpu.VMEM((LANES, LANES), f32),
            pltpu.VMEM((32, LANES), f32),
            pltpu.VMEM((planes_all, 2, LANES), f32),
            pltpu.VMEM((planes_all, 2, LANES), f32),
            pltpu.VMEM((2, 2 * SUB, LANES), f32),
            pltpu.VMEM((2, 2 * SUB, LANES), f32),
            pltpu.VMEM((2, 2 * SUB, LANES), f32),
            pltpu.VMEM((2, 2, 2 * SUB, LANES), f32),
            pltpu.VMEM((B, 1, LANES), f32),
            pltpu.VMEM((B, 3, LANES), f32),
            pltpu.VMEM((B, NODE_DEV, LANES), bf16),
            dma((9,)),
            dma, dma((T,)),
            dma, dma,
            dma, dma,
            dma, dma((2,)),
            dma((2,)), dma((2, 2)),
            dma((2,)), dma((2, T)),
            dma((2,)), dma((2, 2)),
            dma((2,)), dma((2, 2)),
            dma((2,)), dma((2, 2)),
        ],
        compiler_params=pltpu.CompilerParams(collective_id=0, has_side_effects=True),
        name="flutter",
    )(jac_blocks[0], psi_start[0, :, 0], source[0, :, 0], pseudo_step[0, 0], dissipation[0, 0],
      freq_volume[0, 0], normals[0], face_owner[:, :, 0], face_slot)
    adj = pltpu.with_memory_space_constraint(adj, pltpu.VMEM)
    sens = pltpu.with_memory_space_constraint(sens, pltpu.VMEM)
    adj, sens = pl.pallas_call(
        hand_over,
        out_shape=(
            jax.ShapeDtypeStruct(field, f32),
            jax.ShapeDtypeStruct((6, 1, NODE_DEV), f32),
        ),
        in_specs=[vm, vm],
        out_specs=(hbm, hbm),
        scratch_shapes=[
            dma((2,)),
        ],
        name="hand_over",
    )(adj, sens)
    return adj[None, :, None], jnp.transpose(sens, (1, 0, 2))


def solution(mesh):
    placed = (
        P("passage", None, None, "brick"),
        P("passage", None, "brick", None, None),
        P("passage", None, "brick", None, None),
        P("passage", "brick", None, None),
        P("passage", "brick", None, None),
        P("passage", "brick", None, None),
        P("passage", None, "brick", None),
        P("passage", "brick", None),
        P("passage", "brick"),
    )
    return jax.shard_map(
        functools.partial(body, mesh.shape["brick"], mesh.shape["passage"]),
        mesh=mesh,
        in_specs=placed,
        out_specs=(P("passage", None, "brick", None, None), P("passage", None, "brick")),
        check_vma=False,
    )
```

```python
import functools
import math

import jax
import jax.numpy as jnp
from jax import lax
from jax.experimental import pallas as pl
from jax.experimental.pallas import tpu as pltpu
from jax.sharding import PartitionSpec as P

NODE_DEV = 256
SWEEPS = 2
ND = 1
BLADES = 36
LANES = 128
SUB = 8
CODE = 32767.0
BOUND = 6.0
MESH = pl.DeviceIdType.MESH


def flip(index, mask, count):
    other = index
    for b in range(count.bit_length() - 1):
        if mask >> b & 1:
            other = other + (1 << b) * (1 - 2 * lax.rem(lax.div(index, 1 << b), 2))
    return other


def kernel(
    B, passes, phase_angle,
    jac_h, psi_h, source_h, pstep_h, diss_h, freq_h, normals_h, owner_h, slot_h,
    adj, sens,
    jac, source, pstep, diss, freq, normals_v, owner, slot,
    jpack, jsend, jrecv, jflat, pad0, pad1,
    code0, low0, high0, code1, low1, high1, rim_send, rim_recv,
    mix, turned, stage, jturn, jwall, jw_send, jw_recv,
    wall, wall_low, wall_high, wall_rim, idbuf, valbuf, hits,
    l_s, j_s, j_r, jw_s, jw_r, i_s, i_r, v_s, v_r,
    h_s, h_r, g_s, g_r, w_s, w_r, r_s, r_r, q_s, q_r,
):
    me = lax.axis_index("brick")
    mp = lax.axis_index("passage")
    NJ, NK = source.shape[1], source.shape[2]
    R = jac.shape[2] // LANES
    planes = jac.shape[1]
    rows = 25 * R
    pitch = jpack.shape[0] // planes
    T = NJ // SUB
    G = SUB // R
    mine = lax.div(me, G)
    up_p = lax.rem(mp + 1, passes)
    down_p = lax.rem(mp + passes - 1, passes)
    f32 = jnp.float32

    barrier = pltpu.get_barrier_semaphore()
    for d in range(1, B):
        pl.semaphore_signal(
            barrier, inc=1, device_id={"brick": lax.rem(me + d, B)}, device_id_type=MESH
        )
    pl.semaphore_signal(barrier, inc=1, device_id={"passage": up_p}, device_id_type=MESH)
    greeted = B
    if passes > 2:
        pl.semaphore_signal(barrier, inc=1, device_id={"passage": down_p}, device_id_type=MESH)
        greeted += 1

    psi = pad0.at[:, pl.ds(SUB, NJ), :]
    loads = [
        pltpu.make_async_copy(src, dst, l_s.at[k])
        for k, (src, dst) in enumerate((
            (psi_h, psi), (jac_h, jac), (owner_h, owner), (slot_h, slot), (normals_h, normals_v),
            (source_h, source), (pstep_h, pstep), (diss_h, diss), (freq_h, freq),
        ))
    ]
    for load in loads:
        load.start()

    @pl.when(me == 0)
    def _():
        low0[...] = jnp.zeros_like(low0)
        low1[...] = jnp.zeros_like(low1)
        wall_low[...] = jnp.zeros_like(wall_low)

    @pl.when(me == B - 1)
    def _():
        high0[...] = jnp.zeros_like(high0)
        high1[...] = jnp.zeros_like(high1)
        wall_high[...] = jnp.zeros_like(wall_high)

    def copy_to(src, dst, send, recv, axis, peer):
        return pltpu.make_async_remote_copy(
            src_ref=src, dst_ref=dst, send_sem=send, recv_sem=recv,
            device_id={axis: peer}, device_id_type=MESH,
        )

    def beside_copies(src, low, high, send, recv):
        up = copy_to(src, low, send.at[0], recv[0], "brick", lax.rem(me + 1, B))
        down = copy_to(src, high, send.at[1], recv[1], "brick", lax.rem(me + B - 1, B))
        return up, down

    def beside_start(up, down):
        @pl.when(me < B - 1)
        def _():
            up.start()

        @pl.when(me > 0)
        def _():
            down.start()

    def beside_recv(up, down):
        @pl.when(me > 0)
        def _():
            up.wait_recv()

        @pl.when(me < B - 1)
        def _():
            down.wait_recv()

    def await_bytes(ref, sem):
        pltpu.make_async_copy(ref, ref, sem).wait()

    def beside_sent(ref, send):
        @pl.when(me < B - 1)
        def _():
            await_bytes(ref, send.at[0])

        @pl.when(me > 0)
        def _():
            await_bytes(ref, send.at[1])

    lanes = lax.broadcasted_iota(jnp.int32, (NJ, NK), 1)
    lane = lax.broadcasted_iota(jnp.int32, (1, LANES), 1)
    sub = lax.broadcasted_iota(jnp.int32, (SUB, NK), 0)
    lane8 = lax.broadcasted_iota(jnp.int32, (SUB, NK), 1)

    def turn_over(slot, pieces):
        halves = [jnp.zeros((NJ, NK), f32), jnp.zeros((NJ, NK), f32)]
        for to, columns, load in pieces:
            x = jnp.concatenate([load(r) for r in range(R)], axis=0) if R > 1 else load(0)
            for half, column in enumerate(columns):
                if column is not None:
                    shift = (to - column) % NK
                    y = pltpu.roll(x, shift, 1) if shift else x
                    halves[half] = jnp.where(lanes == to, y, halves[half])
        turned[slot, :, :] = jnp.concatenate(halves, axis=0).T

    def plane_rows(ref):
        return lambda r: ref[pl.ds(r, B, stride=R), :]

    def field_rows(ref, c, shift):
        return lambda r: ref[c, pl.ds(shift + r, B, stride=R), :]

    def spread(c):
        return c + c // 5 * 3

    loads[0].wait()
    for k, row in enumerate((SUB + NJ - 1, SUB)):
        for c in range(10):
            rim_send[0, k, pl.ds(c, 1), :] = pad0[c, pl.ds(row, 1), :]
    turn_over(
        0,
        [(spread(c), (0, 1), field_rows(pad0, c, SUB)) for c in range(10)]
        + [(2 * SUB + spread(c), (None, 2), field_rows(pad0, c, SUB)) for c in range(10)],
    )
    wall[0, :, :] = turned[0, 0 : 2 * SUB, :]
    for t in range(T):
        for c in range(0, 10, 2):
            at = pl.ds(SUB + t * SUB, SUB)
            x = jnp.concatenate([pad0[c, at, :], pad0[c + 1, at, :]], axis=0)
            q = jnp.round(x * (CODE / BOUND))
            code0[t, pl.ds(c * SUB, 2 * SUB), :] = q.astype(jnp.int32).astype(jnp.int16)

    loads[1].wait()
    for n in range(25):
        for r in range(R):
            for g in range(planes // SUB):
                x = jac[n, pl.ds(g * SUB, SUB), pl.ds(r * LANES, LANES)].astype(f32)
                jpack[pl.ds(g * SUB * pitch + r * 25 + n, SUB, stride=pitch), :] = x
    first = lax.broadcasted_iota(jnp.int32, (SUB, LANES), 0) == lane
    first = jnp.where(first, 1.0, 0.0).astype(jnp.bfloat16)
    for p in range(planes):
        x = jpack[pl.ds(p * pitch, pitch), :]
        jsend[p, :, :] = x[0:rows].astype(jnp.bfloat16)
        x = jnp.concatenate([x, jnp.zeros((LANES - pitch, LANES), f32)], axis=0)
        y = lax.dot_general(
            first, x.astype(jnp.bfloat16), (((1,), (1,)), ((), ())), preferred_element_type=f32
        )
        jw_send[p, :, :] = y[0:2]

    j_copies, jw_copies, id_copies, val_copies = [], [], [], []
    for d in list(range(B // 2, B)) + list(range(1, B // 2))[::-1]:
        peer = flip(me, d, B)
        j_copies.append(
            copy_to(jsend.at[peer], jrecv.at[me], j_s, j_r.at[mine], "brick", peer)
        )
        jw_copies.append(copy_to(jw_send.at[peer], jw_recv.at[me], jw_s, jw_r, "brick", peer))
        id_copies.append(copy_to(idbuf.at[me], idbuf.at[me], i_s, i_r, "brick", peer))
        val_copies.append([
            copy_to(valbuf.at[me], valbuf.at[me], v_s, v_r.at[k], "brick", peer) for k in range(2)
        ])

    centres = (B // 2 - 1, B // 2)
    central = jnp.logical_or(me == centres[0], me == centres[1])

    def rim_copies(sweep):
        return [
            copy_to(
                rim_send.at[sweep, k], rim_recv.at[sweep, k], r_s.at[k], r_r.at[sweep, k],
                "passage", peer,
            )
            for k, peer in ((0, up_p), (1, down_p))
        ]

    def wall_rims(sweep):
        return [
            copy_to(
                wall.at[sweep], wall_rim.at[sweep, k], q_s.at[k], q_r.at[sweep, k],
                "passage", peer,
            )
            for k, peer in ((0, up_p), (1, down_p))
        ]

    def wall_copies(sweep):
        return beside_copies(
            wall.at[sweep], wall_low.at[sweep], wall_high.at[sweep], w_s,
            (w_r.at[sweep, 0], w_r.at[sweep, 1]),
        )

    def tile_copies(t):
        return beside_copies(
            code1.at[t], low1.at[t], high1.at[t], g_s, (g_r.at[0, t], g_r.at[1, t])
        )

    rims0, rims1 = rim_copies(0), rim_copies(1)
    half = T // 2
    upper = lax.div(mine, half)

    def side_of(brick):
        return lax.div(lax.div(brick, G), half)

    def halo_copies(k):
        copies = []
        for step, dst in ((1, low0), (B - 1, high0)):
            peer = lax.rem(me + step, B)
            side = side_of(peer)
            part = side if k == 0 else 1 - side
            at = pl.ds(part * half, half)
            copies.append(copy_to(
                code0.at[at], dst.at[at], h_s.at[0 if step == 1 else 1],
                h_r.at[0 if step == 1 else 1, k], "brick", peer,
            ))
        return copies

    def halo_recv(k):
        part = upper if k == 0 else 1 - upper
        at = pl.ds(part * half, half)

        @pl.when(me > 0)
        def _():
            await_bytes(low0.at[at], h_r.at[0, k])

        @pl.when(me < B - 1)
        def _():
            await_bytes(high0.at[at], h_r.at[1, k])

    pl.semaphore_wait(barrier, greeted)
    for copy in wall_rims(0) + rims0:
        copy.start()
    beside_start(*wall_copies(0))
    for copy in jw_copies:
        copy.start()
    beside_start(*halo_copies(0))
    for copy in j_copies[: B // 8] + j_copies[B // 2 :] + j_copies[B // 8 : B // 4]:
        copy.start()
    beside_start(*halo_copies(1))

    jrecv[pl.ds(me, 1), :, :] = jsend[pl.ds(me, 1), :, :]
    jw_recv[pl.ds(me, 1), :, :] = jw_send[pl.ds(me, 1), :, :]
    for load in loads[5:]:
        load.wait()
    turn_over(
        1,
        [(k, (0, 1), plane_rows(ref)) for k, ref in enumerate((pstep, diss, freq))]
        + [(SUB + spread(c), (0, 1), field_rows(source, c, 0)) for c in range(10)],
    )

    for k in (2, 3, 4):
        loads[k].wait()
    faces = owner.shape[1]
    mix[...] = jnp.zeros_like(mix)
    mix[0:1, pl.ds(0, faces)] = (owner[...] * NODE_DEV + slot[...]).astype(f32)
    for d in range(3):
        mix[1 + d : 2 + d, pl.ds(0, faces)] = normals_v[d, :, :]
    stage[...] = jnp.concatenate(
        [mix[...], jnp.zeros((LANES - SUB, LANES), f32)], axis=0
    ).T
    x = [stage[pl.ds(r, B, stride=R), :] for r in range(R)]
    mix[...] = jnp.concatenate(x + x, axis=0).T[0:SUB]
    idbuf[pl.ds(me, 1), :, :] = mix[0:1, :].reshape(1, 1, LANES)
    for copy in id_copies:
        copy.start()

    def rotated(re, im, edge, turn):
        at_edge = mp == edge
        cosine = jnp.where(at_edge, math.cos(turn), 1.0).astype(f32)
        sine = jnp.where(at_edge, math.sin(turn), 0.0).astype(f32)
        return re * cosine - im * sine, re * sine + im * cosine

    def place_rim(sweep, pad, k):
        edge, turn, row = ((0, -phase_angle, SUB - 1), (passes - 1, phase_angle, SUB + NJ))[k]
        rim = rim_recv[sweep, k, :, :]
        parts = rotated(rim[0:5], rim[5:10], edge, turn)
        for c in range(10):
            pad[c, pl.ds(row, 1), :] = parts[c // 5][c % 5 : c % 5 + 1]

    def tile_step(t, pad, low, high, sweep):
        at = pl.ds(pl.multiple_of(t * SUB, SUB), SUB)
        here = pl.ds(pl.multiple_of(t * SUB + SUB, SUB), SUB)
        after = pl.ds(pl.multiple_of(t * SUB + 2 * SUB, SUB), SUB)
        om, ds_, ps = freq[at, :], diss[at, :], pstep[at, :]
        us = [pad[c, here, :] for c in range(10)]
        sides = []
        for ref in (low, high):
            if sweep == 0:
                scale = BOUND / CODE
            else:
                scale = ref[t, pl.ds(10 * SUB, 2), :].astype(jnp.int32).astype(f32)[0:1]
                scale = scale * (1.0 / (256.0 * CODE))
            side = []
            for c in range(0, 10, 2):
                x = ref[t, pl.ds(c * SUB, 2 * SUB), :].astype(jnp.int32).astype(f32)
                side += [x[0:SUB] * scale, x[SUB : 2 * SUB] * scale]
            sides.append(side)
        lows, highs = sides
        diff = [0.5 * (h - l) for h, l in zip(highs, lows)]
        conv = [None] * 10
        for n in range(5):
            for m in range(5):
                tile = jflat[t, pl.ds(n * 5 + m, SUB, stride=25), :]
                for part in (0, 5):
                    term = tile * diff[part + n]
                    conv[part + m] = term if conv[part + m] is None else conv[part + m] + term
        fresh = []
        for c in range(10):
            u = us[c]
            above = jnp.where(
                sub == SUB - 1, pltpu.roll(pad[c, after, :], SUB - 1, 0), pltpu.roll(u, SUB - 1, 0)
            )
            below = jnp.where(sub == 0, pltpu.roll(pad[c, at, :], 1, 0), pltpu.roll(u, 1, 0))
            beside = highs[c] + lows[c] + above + below
            beside = beside + jnp.where(lane8 == NK - 1, 0.0, pltpu.roll(u, NK - 1, 1))
            beside = beside + jnp.where(lane8 == 0, 0.0, pltpu.roll(u, 1, 1))
            spin = om * us[c + 5] if c < 5 else -(om * us[c - 5])
            resid = conv[c] + spin + ds_ * (6.0 * u - beside) - source[c, at, :]
            fresh.append(u - ps * resid)
        return fresh

    def first_step(u):
        t = flip(mine, u, T)
        @pl.when(t == 0)
        def _():
            rims0[0].wait_recv()
            place_rim(0, pad0, 0)

        @pl.when(t == T - 1)
        def _():
            rims0[1].wait_recv()
            place_rim(0, pad0, 1)

        count = G if u else G - 1
        if count:
            await_bytes(jrecv.at[pl.ds(0, count)], j_r.at[t])
        for g in range(G):
            jflat[t, pl.ds(g * rows, rows), :] = jrecv[t * G + g, :, :].astype(f32)
        fresh = tile_step(t, pad0, low0, high0, 0)
        here = pl.ds(pl.multiple_of(t * SUB + SUB, SUB), SUB)
        top = jnp.abs(fresh[0])
        for c in range(10):
            pad1[c, here, :] = fresh[c]
            top = jnp.maximum(top, jnp.abs(fresh[c]))
        for k, (tile, row) in enumerate(((T - 1, SUB - 1), (0, 0))):
            @pl.when(t == tile)
            def _():
                for c in range(10):
                    rim_send[1, k, pl.ds(c, 1), :] = fresh[c][row : row + 1]
                rims1[k].start()

        top = jnp.floor(jnp.max(top, axis=0, keepdims=True) * 256.0) + 1.0
        top = jnp.broadcast_to(top, (2 * SUB, NK))
        scale = (256.0 * CODE) / top
        for c in range(0, 10, 2):
            x = jnp.concatenate([fresh[c], fresh[c + 1]], axis=0)
            q = jnp.round(x * scale)
            code1[t, pl.ds(c * SUB, 2 * SUB), :] = q.astype(jnp.int32).astype(jnp.int16)
        code1[t, pl.ds(10 * SUB, 2), :] = top[0:2].astype(jnp.int32).astype(jnp.int16)
        beside_start(*tile_copies(t))

    def second_step(t):
        @pl.when(t == 0)
        def _():
            rims1[0].wait_recv()
            place_rim(1, pad1, 0)

        @pl.when(t == T - 1)
        def _():
            rims1[1].wait_recv()
            place_rim(1, pad1, 1)

        beside_recv(*tile_copies(t))
        fresh = tile_step(t, pad1, low1, high1, 1)
        for c in range(10):
            adj[c, pl.ds(pl.multiple_of(t * SUB, SUB), SUB), :] = fresh[c]

    place = lax.rem(lane, NJ)
    turn_of = lax.div(place, B)

    def wall_step(sweep):
        u16, low16, high16 = wall[sweep, :, :], wall_low[sweep, :, :], wall_high[sweep, :, :]
        fold = (R - 1) * B - 1

        def moved(x, shift):
            shift = shift % LANES
            return pltpu.roll(x, shift, 1) if shift else x

        rims = []
        for k, (edge, turn, shift) in enumerate((
            (0, -phase_angle, 1 - NJ), (passes - 1, phase_angle, NJ - 1),
        )):
            rim = moved(wall_rim[sweep, k, :, :], shift)
            rims.append(rotated(rim[0:5], rim[SUB : SUB + 5], edge, turn))
        out = []
        for part in range(2):
            at = slice(SUB * part, SUB * part + 5)
            other = slice(SUB * (1 - part), SUB * (1 - part) + 5)
            u, lo, hi = u16[at], low16[at], high16[at]
            diff = 0.5 * (hi - lo)
            conv = jwall[0:5, :] * diff[0:1]
            for n in range(1, 5):
                conv = conv + jwall[pl.ds(5 * n, 5), :] * diff[n : n + 1]
            below = jnp.where(turn_of == 0, moved(u, -fold), moved(u, B))
            below = jnp.where(place == 0, rims[0][part], below)
            above = jnp.where(turn_of == R - 1, moved(u, fold), moved(u, -B))
            above = jnp.where(place == NJ - 1, rims[1][part], above)
            beside = hi + lo + above + below + moved(u, NJ)
            if sweep == 0:
                second = turned[0, pl.ds(2 * SUB + SUB * part, 5), :]
                beside = beside + jnp.where(lane < NJ, 0.0, second)
            spin = turned[1, 2:3, :] * u16[other]
            spin = -spin if part else spin
            resid = conv + spin + turned[1, 1:2, :] * (6.0 * u - beside)
            resid = resid - turned[1, pl.ds(SUB + SUB * part, 5), :]
            out.append(u - turned[1, 0:1, :] * resid)
        return out

    def wall_first():
        beside_recv(*wall_copies(0))
        for copy in wall_rims(0):
            copy.wait_recv()
        await_bytes(jw_recv.at[pl.ds(0, B - 1)], jw_r)
        for s in range(B):
            for k in range(2):
                stage[pl.ds(k * B + s, 1), :] = jw_recv[s, pl.ds(k, 1), :]
        jturn[...] = stage[...].T
        total = jnp.zeros((32, LANES), f32)
        for k in range(2):
            for r in range(R):
                x = jturn[pl.ds(r * 25, 32), :]
                shift = k * (NJ - B) + r * B
                x = pltpu.roll(x, shift, 1) if shift else x
                start = k * NJ + r * B
                total = jnp.where((lane >= start) & (lane < start + B), x, total)
        jwall[...] = total
        wall[1, :, :] = jnp.zeros((2 * SUB, LANES), f32)
        for part, fresh in enumerate(wall_step(0)):
            wall[1, pl.ds(SUB * part, 5), :] = fresh
        for copy in wall_rims(1):
            copy.start()
        beside_start(*wall_copies(1))

    def wall_second():
        beside_recv(*wall_copies(1))
        for copy in wall_rims(1):
            copy.wait_recv()
        sides = mix[1:4, :]
        real, imag = [fresh[1:4] * sides for fresh in wall_step(1)]
        both = jnp.where(lane < NJ, real, pltpu.roll(imag, NJ, 1))
        valbuf[pl.ds(me, 1), :, :] = both[None]

        @pl.when(central)
        def _():
            for copies in val_copies:
                copies[1].start()

        @pl.when(jnp.logical_not(central))
        def _():
            for copies in val_copies:
                copies[0].start()

    def gather_hits():
        await_bytes(idbuf.at[pl.ds(0, B - 1)], i_r)
        node = lax.broadcasted_iota(jnp.int32, (NODE_DEV, LANES), 0) + me * NODE_DEV
        node = node.astype(f32)
        for s in range(B):
            hits[s, :, :] = jnp.where(idbuf[s, :, :] == node, 1.0, 0.0).astype(jnp.bfloat16)

    def sum_nodes(late, total):
        @pl.when(central)
        def _():
            await_bytes(valbuf.at[pl.ds(0, 1 if late else B - 2)], v_r.at[late])

        @pl.when(jnp.logical_not(central))
        def _():
            await_bytes(valbuf.at[pl.ds(0, 2 if late else B - 3)], v_r.at[late])

        for s in centres if late else [s for s in range(B) if s not in centres]:
            v = valbuf[s, :, :]
            v = jnp.concatenate(
                [jnp.where(lane < NJ, v, 0.0), jnp.where(lane < NJ, 0.0, v), jnp.zeros((2, LANES), f32)],
                axis=0,
            )
            a = v.astype(jnp.bfloat16).astype(f32)
            rest = v - a
            b = rest.astype(jnp.bfloat16).astype(f32)
            parts = jnp.concatenate([a, b, rest - b], axis=0).astype(jnp.bfloat16)
            total = total + lax.dot_general(
                parts, hits[s, :, :], (((1,), (1,)), ((), ())), preferred_element_type=f32
            )
        return total

    spot = lax.rem(mine, half)

    def differ(p, q):
        out = 0
        for b in range(half.bit_length() - 1):
            one = lax.rem(lax.div(p, 1 << b) + lax.div(q, 1 << b), 2)
            out = out + (1 << b) * one
        return out

    def near_tile(i):
        return half - 1 - i + upper * (1 + 2 * i)

    def far_tile(i):
        outer = (1 - upper) * (half - 1)
        turn = differ(spot, outer)
        if i < half - 1:
            turn = i + lax.div(i + half - turn, half)
        return (1 - upper) * half + differ(spot, turn)

    wall_first()
    for copy in j_copies[B // 4 : B // 2]:
        copy.start()
    halo_recv(0)
    for u in range(half):
        first_step(u)
    wall_second()
    halo_recv(1)
    first_step(half)
    for u in range(half + 1, T):
        first_step(u)
    gather_hits()
    total = sum_nodes(0, jnp.zeros((3 * SUB, NODE_DEV), f32))
    for i in range(half - 1):
        second_step(near_tile(i))
    for i in range(half - 1):
        second_step(far_tile(i))
    second_step(near_tile(half - 1))
    second_step(far_tile(half - 1))
    total = sum_nodes(1, total)
    summed = total[0:SUB] + total[SUB : 2 * SUB] + total[2 * SUB :]
    sens[...] = summed[0:6].reshape(6, 1, NODE_DEV)
    await_bytes(jsend.at[pl.ds(0, B - 1)], j_s)
    await_bytes(jw_send.at[pl.ds(0, B - 1)], jw_s)
    await_bytes(idbuf.at[pl.ds(0, B - 1)], i_s)
    await_bytes(valbuf.at[pl.ds(0, B - 1)], v_s)
    for k in range(2):
        await_bytes(rim_send.at[k], r_s.at[k])
        await_bytes(wall, q_s.at[k])
    beside_sent(code0, h_s)
    beside_sent(code1, g_s)
    beside_sent(wall, w_s)


def hand_over(adj, sens, adj_out, sens_out, out_s):
    outs = [pltpu.make_async_copy(adj, adj_out, out_s.at[0]), pltpu.make_async_copy(sens, sens_out, out_s.at[1])]
    for copy in outs:
        copy.start()
    for copy in outs:
        copy.wait()


def body(B, passes, jac_blocks, psi_start, source, pseudo_step, dissipation, freq_volume,
         normals, face_owner, face_slot):
    _, _, planes_all, cells = jac_blocks.shape
    NJ, NK = psi_start.shape[3:]
    phase_angle = 2.0 * math.pi * ND * passes / BLADES
    R = cells // LANES
    rows = 25 * R
    pitch = -(-rows // SUB) * SUB
    faces = face_slot.shape[1]
    T = NJ // SUB
    f32 = jnp.float32
    i16 = jnp.int16
    bf16 = jnp.bfloat16
    field, plane = (10, NJ, NK), (NJ, NK)
    coded, scaled = (T, 10 * SUB, NK), (T, 10 * SUB + 2, NK)
    hbm = pl.BlockSpec(memory_space=pl.ANY)
    vm = pl.BlockSpec(memory_space=pltpu.VMEM)
    dma = pltpu.SemaphoreType.DMA
    adj, sens = pl.pallas_call(
        functools.partial(kernel, B, passes, phase_angle),
        out_shape=(
            pltpu.VMEM(field, f32),
            pltpu.VMEM((6, 1, NODE_DEV), f32),
        ),
        in_specs=[hbm] * 9,
        out_specs=(vm, vm),
        scratch_shapes=[
            pltpu.VMEM((25, planes_all, cells), bf16),
            pltpu.VMEM(field, f32),
            pltpu.VMEM(plane, f32),
            pltpu.VMEM(plane, f32),
            pltpu.VMEM(plane, f32),
            pltpu.VMEM((3, 1, faces), f32),
            pltpu.VMEM((1, faces), jnp.int32),
            pltpu.VMEM((1, faces), jnp.int32),
            pltpu.VMEM((planes_all * pitch, LANES), f32),
            pltpu.VMEM((planes_all, rows, LANES), bf16),
            pltpu.VMEM((planes_all, rows, LANES), bf16),
            pltpu.VMEM((T, 25 * SUB, LANES), f32),
            pltpu.VMEM((10, NJ + 2 * SUB, NK), f32),
            pltpu.VMEM((10, NJ + 2 * SUB, NK), f32),
            pltpu.VMEM(coded, i16),
            pltpu.VMEM(coded, i16),
            pltpu.VMEM(coded, i16),
            pltpu.VMEM(scaled, i16),
            pltpu.VMEM(scaled, i16),
            pltpu.VMEM(scaled, i16),
            pltpu.VMEM((2, 2, 2 * SUB, NK), f32),
            pltpu.VMEM((2, 2, 2 * SUB, NK), f32),
            pltpu.VMEM((SUB, LANES), f32),
            pltpu.VMEM((2, LANES, LANES), f32),
            pltpu.VMEM((LANES, LANES), f32),
            pltpu.VMEM((LANES, LANES), f32),
            pltpu.VMEM((32, LANES), f32),
            pltpu.VMEM((planes_all, 2, LANES), f32),
            pltpu.VMEM((planes_all, 2, LANES), f32),
            pltpu.VMEM((2, 2 * SUB, LANES), f32),
            pltpu.VMEM((2, 2 * SUB, LANES), f32),
            pltpu.VMEM((2, 2 * SUB, LANES), f32),
            pltpu.VMEM((2, 2, 2 * SUB, LANES), f32),
            pltpu.VMEM((B, 1, LANES), f32),
            pltpu.VMEM((B, 3, LANES), f32),
            pltpu.VMEM((B, NODE_DEV, LANES), bf16),
            dma((9,)),
            dma, dma((T,)),
            dma, dma,
            dma, dma,
            dma, dma((2,)),
            dma((2,)), dma((2, 2)),
            dma((2,)), dma((2, T)),
            dma((2,)), dma((2, 2)),
            dma((2,)), dma((2, 2)),
            dma((2,)), dma((2, 2)),
        ],
        compiler_params=pltpu.CompilerParams(collective_id=0, has_side_effects=True),
        name="flutter",
    )(jac_blocks[0], psi_start[0, :, 0], source[0, :, 0], pseudo_step[0, 0], dissipation[0, 0],
      freq_volume[0, 0], normals[0], face_owner[:, :, 0], face_slot)
    adj = pltpu.with_memory_space_constraint(adj, pltpu.VMEM)
    sens = pltpu.with_memory_space_constraint(sens, pltpu.VMEM)
    adj, sens = pl.pallas_call(
        hand_over,
        out_shape=(
            jax.ShapeDtypeStruct(field, f32),
            jax.ShapeDtypeStruct((6, 1, NODE_DEV), f32),
        ),
        in_specs=[vm, vm],
        out_specs=(hbm, hbm),
        scratch_shapes=[
            dma((2,)),
        ],
        name="hand_over",
    )(adj, sens)
    return adj[None, :, None], jnp.transpose(sens, (1, 0, 2))


def solution(mesh):
    placed = (
        P("passage", None, None, "brick"),
        P("passage", None, "brick", None, None),
        P("passage", None, "brick", None, None),
        P("passage", "brick", None, None),
        P("passage", "brick", None, None),
        P("passage", "brick", None, None),
        P("passage", None, "brick", None),
        P("passage", "brick", None),
        P("passage", "brick"),
    )
    return jax.shard_map(
        functools.partial(body, mesh.shape["brick"], mesh.shape["passage"]),
        mesh=mesh,
        in_specs=placed,
        out_specs=(P("passage", None, "brick", None, None), P("passage", None, "brick")),
        check_vma=False,
    )
```

```python
import functools
import math

import jax
import jax.numpy as jnp
from jax import lax
from jax.experimental import pallas as pl
from jax.experimental.pallas import tpu as pltpu
from jax.sharding import PartitionSpec as P

NODE_DEV = 256
SWEEPS = 2
ND = 1
BLADES = 36
LANES = 128
SUB = 8
CODE = 32767.0
BOUND = 6.0
MESH = pl.DeviceIdType.MESH


def flip(index, mask, count):
    other = index
    for b in range(count.bit_length() - 1):
        if mask >> b & 1:
            other = other + (1 << b) * (1 - 2 * lax.rem(lax.div(index, 1 << b), 2))
    return other


def kernel(
    B, passes, phase_angle,
    jac_h, psi_h, source_h, pstep_h, diss_h, freq_h, normals_h, owner_h, slot_h,
    adj, sens,
    jac, source, pstep, diss, freq, normals_v, owner, slot,
    jpack, jsend, jrecv, jflat, pad0, pad1,
    code0, low0, high0, code1, low1, high1, rim_send, rim_recv,
    mix, turned, stage, jturn, jwall, jw_send, jw_recv,
    wall, wall_low, wall_high, wall_rim, idbuf, valbuf, hits,
    l_s, j_s, j_r, jw_s, jw_r, i_s, i_r, v_s, v_r,
    h_s, h_r, g_s, g_r, w_s, w_r, r_s, r_r, q_s, q_r,
):
    me = lax.axis_index("brick")
    mp = lax.axis_index("passage")
    NJ, NK = source.shape[1], source.shape[2]
    R = jac.shape[2] // LANES
    planes = jac.shape[1]
    rows = 25 * R
    pitch = jpack.shape[0] // planes
    T = NJ // SUB
    G = SUB // R
    mine = lax.div(me, G)
    up_p = lax.rem(mp + 1, passes)
    down_p = lax.rem(mp + passes - 1, passes)
    f32 = jnp.float32

    barrier = pltpu.get_barrier_semaphore()
    for d in range(1, B):
        pl.semaphore_signal(
            barrier, inc=1, device_id={"brick": lax.rem(me + d, B)}, device_id_type=MESH
        )
    pl.semaphore_signal(barrier, inc=1, device_id={"passage": up_p}, device_id_type=MESH)
    greeted = B
    if passes > 2:
        pl.semaphore_signal(barrier, inc=1, device_id={"passage": down_p}, device_id_type=MESH)
        greeted += 1

    psi = pad0.at[:, pl.ds(SUB, NJ), :]
    loads = [
        pltpu.make_async_copy(src, dst, l_s.at[k])
        for k, (src, dst) in enumerate((
            (psi_h, psi), (jac_h, jac), (owner_h, owner), (slot_h, slot), (normals_h, normals_v),
            (source_h, source), (pstep_h, pstep), (diss_h, diss), (freq_h, freq),
        ))
    ]
    for load in loads:
        load.start()

    @pl.when(me == 0)
    def _():
        low0[...] = jnp.zeros_like(low0)
        low1[...] = jnp.zeros_like(low1)
        wall_low[...] = jnp.zeros_like(wall_low)

    @pl.when(me == B - 1)
    def _():
        high0[...] = jnp.zeros_like(high0)
        high1[...] = jnp.zeros_like(high1)
        wall_high[...] = jnp.zeros_like(wall_high)

    def copy_to(src, dst, send, recv, axis, peer):
        return pltpu.make_async_remote_copy(
            src_ref=src, dst_ref=dst, send_sem=send, recv_sem=recv,
            device_id={axis: peer}, device_id_type=MESH,
        )

    def beside_copies(src, low, high, send, recv):
        up = copy_to(src, low, send.at[0], recv[0], "brick", lax.rem(me + 1, B))
        down = copy_to(src, high, send.at[1], recv[1], "brick", lax.rem(me + B - 1, B))
        return up, down

    def beside_start(up, down):
        @pl.when(me < B - 1)
        def _():
            up.start()

        @pl.when(me > 0)
        def _():
            down.start()

    def beside_recv(up, down):
        @pl.when(me > 0)
        def _():
            up.wait_recv()

        @pl.when(me < B - 1)
        def _():
            down.wait_recv()

    def await_bytes(ref, sem):
        pltpu.make_async_copy(ref, ref, sem).wait()

    def beside_sent(ref, send):
        @pl.when(me < B - 1)
        def _():
            await_bytes(ref, send.at[0])

        @pl.when(me > 0)
        def _():
            await_bytes(ref, send.at[1])

    lanes = lax.broadcasted_iota(jnp.int32, (NJ, NK), 1)
    lane = lax.broadcasted_iota(jnp.int32, (1, LANES), 1)
    sub = lax.broadcasted_iota(jnp.int32, (SUB, NK), 0)
    lane8 = lax.broadcasted_iota(jnp.int32, (SUB, NK), 1)

    def turn_over(slot, pieces):
        halves = [jnp.zeros((NJ, NK), f32), jnp.zeros((NJ, NK), f32)]
        for to, columns, load in pieces:
            x = jnp.concatenate([load(r) for r in range(R)], axis=0) if R > 1 else load(0)
            for half, column in enumerate(columns):
                if column is not None:
                    shift = (to - column) % NK
                    y = pltpu.roll(x, shift, 1) if shift else x
                    halves[half] = jnp.where(lanes == to, y, halves[half])
        turned[slot, :, :] = jnp.concatenate(halves, axis=0).T

    def plane_rows(ref):
        return lambda r: ref[pl.ds(r, B, stride=R), :]

    def field_rows(ref, c, shift):
        return lambda r: ref[c, pl.ds(shift + r, B, stride=R), :]

    def spread(c):
        return c + c // 5 * 3

    loads[0].wait()
    for k, row in enumerate((SUB + NJ - 1, SUB)):
        for c in range(10):
            rim_send[0, k, pl.ds(c, 1), :] = pad0[c, pl.ds(row, 1), :]
    turn_over(
        0,
        [(spread(c), (0, 1), field_rows(pad0, c, SUB)) for c in range(10)]
        + [(2 * SUB + spread(c), (None, 2), field_rows(pad0, c, SUB)) for c in range(10)],
    )
    wall[0, :, :] = turned[0, 0 : 2 * SUB, :]
    for t in range(T):
        for c in range(0, 10, 2):
            at = pl.ds(SUB + t * SUB, SUB)
            x = jnp.concatenate([pad0[c, at, :], pad0[c + 1, at, :]], axis=0)
            q = jnp.round(x * (CODE / BOUND))
            code0[t, pl.ds(c * SUB, 2 * SUB), :] = q.astype(jnp.int32).astype(jnp.int16)

    loads[1].wait()
    for n in range(25):
        for r in range(R):
            for g in range(planes // SUB):
                x = jac[n, pl.ds(g * SUB, SUB), pl.ds(r * LANES, LANES)].astype(f32)
                jpack[pl.ds(g * SUB * pitch + r * 25 + n, SUB, stride=pitch), :] = x
    first = lax.broadcasted_iota(jnp.int32, (SUB, LANES), 0) == lane
    first = jnp.where(first, 1.0, 0.0).astype(jnp.bfloat16)
    for p in range(planes):
        x = jpack[pl.ds(p * pitch, pitch), :]
        jsend[p, :, :] = x[0:rows].astype(jnp.bfloat16)
        x = jnp.concatenate([x, jnp.zeros((LANES - pitch, LANES), f32)], axis=0)
        y = lax.dot_general(
            first, x.astype(jnp.bfloat16), (((1,), (1,)), ((), ())), preferred_element_type=f32
        )
        jw_send[p, :, :] = y[0:2]

    j_copies, jw_copies, id_copies, val_copies = [], [], [], []
    for d in list(range(B // 2, B)) + list(range(1, B // 2))[::-1]:
        peer = flip(me, d, B)
        j_copies.append(
            copy_to(jsend.at[peer], jrecv.at[me], j_s, j_r.at[mine], "brick", peer)
        )
        jw_copies.append(copy_to(jw_send.at[peer], jw_recv.at[me], jw_s, jw_r, "brick", peer))
        id_copies.append(copy_to(idbuf.at[me], idbuf.at[me], i_s, i_r, "brick", peer))
        val_copies.append([
            copy_to(valbuf.at[me], valbuf.at[me], v_s, v_r.at[k], "brick", peer) for k in range(2)
        ])

    centres = (B // 2 - 1, B // 2)
    central = jnp.logical_or(me == centres[0], me == centres[1])

    def rim_copies(sweep):
        return [
            copy_to(
                rim_send.at[sweep, k], rim_recv.at[sweep, k], r_s.at[k], r_r.at[sweep, k],
                "passage", peer,
            )
            for k, peer in ((0, up_p), (1, down_p))
        ]

    def wall_rims(sweep):
        return [
            copy_to(
                wall.at[sweep], wall_rim.at[sweep, k], q_s.at[k], q_r.at[sweep, k],
                "passage", peer,
            )
            for k, peer in ((0, up_p), (1, down_p))
        ]

    def wall_copies(sweep):
        return beside_copies(
            wall.at[sweep], wall_low.at[sweep], wall_high.at[sweep], w_s,
            (w_r.at[sweep, 0], w_r.at[sweep, 1]),
        )

    def tile_copies(t):
        return beside_copies(
            code1.at[t], low1.at[t], high1.at[t], g_s, (g_r.at[0, t], g_r.at[1, t])
        )

    rims0, rims1 = rim_copies(0), rim_copies(1)
    half = T // 2
    upper = lax.div(mine, half)

    def side_of(brick):
        return lax.div(lax.div(brick, G), half)

    def halo_copies(k):
        copies = []
        for step, dst in ((1, low0), (B - 1, high0)):
            peer = lax.rem(me + step, B)
            side = side_of(peer)
            part = side if k == 0 else 1 - side
            at = pl.ds(part * half, half)
            copies.append(copy_to(
                code0.at[at], dst.at[at], h_s.at[0 if step == 1 else 1],
                h_r.at[0 if step == 1 else 1, k], "brick", peer,
            ))
        return copies

    def halo_recv(k):
        part = upper if k == 0 else 1 - upper
        at = pl.ds(part * half, half)

        @pl.when(me > 0)
        def _():
            await_bytes(low0.at[at], h_r.at[0, k])

        @pl.when(me < B - 1)
        def _():
            await_bytes(high0.at[at], h_r.at[1, k])

    pl.semaphore_wait(barrier, greeted)
    for copy in wall_rims(0) + rims0:
        copy.start()
    beside_start(*wall_copies(0))
    for copy in jw_copies:
        copy.start()
    beside_start(*halo_copies(0))
    for copy in j_copies[: B // 8] + j_copies[B // 2 :] + j_copies[B // 8 : 3 * B // 16]:
        copy.start()
    beside_start(*halo_copies(1))

    jrecv[pl.ds(me, 1), :, :] = jsend[pl.ds(me, 1), :, :]
    jw_recv[pl.ds(me, 1), :, :] = jw_send[pl.ds(me, 1), :, :]
    for load in loads[5:]:
        load.wait()
    turn_over(
        1,
        [(k, (0, 1), plane_rows(ref)) for k, ref in enumerate((pstep, diss, freq))]
        + [(SUB + spread(c), (0, 1), field_rows(source, c, 0)) for c in range(10)],
    )

    for k in (2, 3, 4):
        loads[k].wait()
    faces = owner.shape[1]
    mix[...] = jnp.zeros_like(mix)
    mix[0:1, pl.ds(0, faces)] = (owner[...] * NODE_DEV + slot[...]).astype(f32)
    for d in range(3):
        mix[1 + d : 2 + d, pl.ds(0, faces)] = normals_v[d, :, :]
    stage[...] = jnp.concatenate(
        [mix[...], jnp.zeros((LANES - SUB, LANES), f32)], axis=0
    ).T
    x = [stage[pl.ds(r, B, stride=R), :] for r in range(R)]
    mix[...] = jnp.concatenate(x + x, axis=0).T[0:SUB]
    idbuf[pl.ds(me, 1), :, :] = mix[0:1, :].reshape(1, 1, LANES)
    for copy in id_copies:
        copy.start()

    def rotated(re, im, edge, turn):
        at_edge = mp == edge
        cosine = jnp.where(at_edge, math.cos(turn), 1.0).astype(f32)
        sine = jnp.where(at_edge, math.sin(turn), 0.0).astype(f32)
        return re * cosine - im * sine, re * sine + im * cosine

    def place_rim(sweep, pad, k):
        edge, turn, row = ((0, -phase_angle, SUB - 1), (passes - 1, phase_angle, SUB + NJ))[k]
        rim = rim_recv[sweep, k, :, :]
        parts = rotated(rim[0:5], rim[5:10], edge, turn)
        for c in range(10):
            pad[c, pl.ds(row, 1), :] = parts[c // 5][c % 5 : c % 5 + 1]

    def tile_step(t, pad, low, high, sweep):
        at = pl.ds(pl.multiple_of(t * SUB, SUB), SUB)
        here = pl.ds(pl.multiple_of(t * SUB + SUB, SUB), SUB)
        after = pl.ds(pl.multiple_of(t * SUB + 2 * SUB, SUB), SUB)
        om, ds_, ps = freq[at, :], diss[at, :], pstep[at, :]
        us = [pad[c, here, :] for c in range(10)]
        sides = []
        for ref in (low, high):
            if sweep == 0:
                scale = BOUND / CODE
            else:
                scale = ref[t, pl.ds(10 * SUB, 2), :].astype(jnp.int32).astype(f32)[0:1]
                scale = scale * (1.0 / (256.0 * CODE))
            side = []
            for c in range(0, 10, 2):
                x = ref[t, pl.ds(c * SUB, 2 * SUB), :].astype(jnp.int32).astype(f32)
                side += [x[0:SUB] * scale, x[SUB : 2 * SUB] * scale]
            sides.append(side)
        lows, highs = sides
        diff = [0.5 * (h - l) for h, l in zip(highs, lows)]
        conv = [None] * 10
        for n in range(5):
            for m in range(5):
                tile = jflat[t, pl.ds(n * 5 + m, SUB, stride=25), :]
                for part in (0, 5):
                    term = tile * diff[part + n]
                    conv[part + m] = term if conv[part + m] is None else conv[part + m] + term
        fresh = []
        for c in range(10):
            u = us[c]
            above = jnp.where(
                sub == SUB - 1, pltpu.roll(pad[c, after, :], SUB - 1, 0), pltpu.roll(u, SUB - 1, 0)
            )
            below = jnp.where(sub == 0, pltpu.roll(pad[c, at, :], 1, 0), pltpu.roll(u, 1, 0))
            beside = highs[c] + lows[c] + above + below
            beside = beside + jnp.where(lane8 == NK - 1, 0.0, pltpu.roll(u, NK - 1, 1))
            beside = beside + jnp.where(lane8 == 0, 0.0, pltpu.roll(u, 1, 1))
            spin = om * us[c + 5] if c < 5 else -(om * us[c - 5])
            resid = conv[c] + spin + ds_ * (6.0 * u - beside) - source[c, at, :]
            fresh.append(u - ps * resid)
        return fresh

    def first_step(u):
        t = flip(mine, u, T)
        @pl.when(t == 0)
        def _():
            rims0[0].wait_recv()
            place_rim(0, pad0, 0)

        @pl.when(t == T - 1)
        def _():
            rims0[1].wait_recv()
            place_rim(0, pad0, 1)

        count = G if u else G - 1
        if count:
            await_bytes(jrecv.at[pl.ds(0, count)], j_r.at[t])
        for g in range(G):
            jflat[t, pl.ds(g * rows, rows), :] = jrecv[t * G + g, :, :].astype(f32)
        fresh = tile_step(t, pad0, low0, high0, 0)
        here = pl.ds(pl.multiple_of(t * SUB + SUB, SUB), SUB)
        top = jnp.abs(fresh[0])
        for c in range(10):
            pad1[c, here, :] = fresh[c]
            top = jnp.maximum(top, jnp.abs(fresh[c]))
        for k, (tile, row) in enumerate(((T - 1, SUB - 1), (0, 0))):
            @pl.when(t == tile)
            def _():
                for c in range(10):
                    rim_send[1, k, pl.ds(c, 1), :] = fresh[c][row : row + 1]
                rims1[k].start()

        top = jnp.floor(jnp.max(top, axis=0, keepdims=True) * 256.0) + 1.0
        top = jnp.broadcast_to(top, (2 * SUB, NK))
        scale = (256.0 * CODE) / top
        for c in range(0, 10, 2):
            x = jnp.concatenate([fresh[c], fresh[c + 1]], axis=0)
            q = jnp.round(x * scale)
            code1[t, pl.ds(c * SUB, 2 * SUB), :] = q.astype(jnp.int32).astype(jnp.int16)
        code1[t, pl.ds(10 * SUB, 2), :] = top[0:2].astype(jnp.int32).astype(jnp.int16)
        beside_start(*tile_copies(t))

    def second_step(t):
        @pl.when(t == 0)
        def _():
            rims1[0].wait_recv()
            place_rim(1, pad1, 0)

        @pl.when(t == T - 1)
        def _():
            rims1[1].wait_recv()
            place_rim(1, pad1, 1)

        beside_recv(*tile_copies(t))
        fresh = tile_step(t, pad1, low1, high1, 1)
        for c in range(10):
            adj[c, pl.ds(pl.multiple_of(t * SUB, SUB), SUB), :] = fresh[c]

    place = lax.rem(lane, NJ)
    turn_of = lax.div(place, B)

    def wall_step(sweep):
        u16, low16, high16 = wall[sweep, :, :], wall_low[sweep, :, :], wall_high[sweep, :, :]
        fold = (R - 1) * B - 1

        def moved(x, shift):
            shift = shift % LANES
            return pltpu.roll(x, shift, 1) if shift else x

        rims = []
        for k, (edge, turn, shift) in enumerate((
            (0, -phase_angle, 1 - NJ), (passes - 1, phase_angle, NJ - 1),
        )):
            rim = moved(wall_rim[sweep, k, :, :], shift)
            rims.append(rotated(rim[0:5], rim[SUB : SUB + 5], edge, turn))
        out = []
        for part in range(2):
            at = slice(SUB * part, SUB * part + 5)
            other = slice(SUB * (1 - part), SUB * (1 - part) + 5)
            u, lo, hi = u16[at], low16[at], high16[at]
            diff = 0.5 * (hi - lo)
            conv = jwall[0:5, :] * diff[0:1]
            for n in range(1, 5):
                conv = conv + jwall[pl.ds(5 * n, 5), :] * diff[n : n + 1]
            below = jnp.where(turn_of == 0, moved(u, -fold), moved(u, B))
            below = jnp.where(place == 0, rims[0][part], below)
            above = jnp.where(turn_of == R - 1, moved(u, fold), moved(u, -B))
            above = jnp.where(place == NJ - 1, rims[1][part], above)
            beside = hi + lo + above + below + moved(u, NJ)
            if sweep == 0:
                second = turned[0, pl.ds(2 * SUB + SUB * part, 5), :]
                beside = beside + jnp.where(lane < NJ, 0.0, second)
            spin = turned[1, 2:3, :] * u16[other]
            spin = -spin if part else spin
            resid = conv + spin + turned[1, 1:2, :] * (6.0 * u - beside)
            resid = resid - turned[1, pl.ds(SUB + SUB * part, 5), :]
            out.append(u - turned[1, 0:1, :] * resid)
        return out

    def wall_first():
        beside_recv(*wall_copies(0))
        for copy in wall_rims(0):
            copy.wait_recv()
        await_bytes(jw_recv.at[pl.ds(0, B - 1)], jw_r)
        for s in range(B):
            for k in range(2):
                stage[pl.ds(k * B + s, 1), :] = jw_recv[s, pl.ds(k, 1), :]
        jturn[...] = stage[...].T
        total = jnp.zeros((32, LANES), f32)
        for k in range(2):
            for r in range(R):
                x = jturn[pl.ds(r * 25, 32), :]
                shift = k * (NJ - B) + r * B
                x = pltpu.roll(x, shift, 1) if shift else x
                start = k * NJ + r * B
                total = jnp.where((lane >= start) & (lane < start + B), x, total)
        jwall[...] = total
        wall[1, :, :] = jnp.zeros((2 * SUB, LANES), f32)
        for part, fresh in enumerate(wall_step(0)):
            wall[1, pl.ds(SUB * part, 5), :] = fresh
        for copy in wall_rims(1):
            copy.start()
        beside_start(*wall_copies(1))

    def wall_second():
        beside_recv(*wall_copies(1))
        for copy in wall_rims(1):
            copy.wait_recv()
        sides = mix[1:4, :]
        real, imag = [fresh[1:4] * sides for fresh in wall_step(1)]
        both = jnp.where(lane < NJ, real, pltpu.roll(imag, NJ, 1))
        valbuf[pl.ds(me, 1), :, :] = both[None]

        @pl.when(central)
        def _():
            for copies in val_copies:
                copies[1].start()

        @pl.when(jnp.logical_not(central))
        def _():
            for copies in val_copies:
                copies[0].start()

    def gather_hits():
        await_bytes(idbuf.at[pl.ds(0, B - 1)], i_r)
        node = lax.broadcasted_iota(jnp.int32, (NODE_DEV, LANES), 0) + me * NODE_DEV
        node = node.astype(f32)
        for s in range(B):
            hits[s, :, :] = jnp.where(idbuf[s, :, :] == node, 1.0, 0.0).astype(jnp.bfloat16)

    def sum_nodes(late, total):
        @pl.when(central)
        def _():
            await_bytes(valbuf.at[pl.ds(0, 1 if late else B - 2)], v_r.at[late])

        @pl.when(jnp.logical_not(central))
        def _():
            await_bytes(valbuf.at[pl.ds(0, 2 if late else B - 3)], v_r.at[late])

        for s in centres if late else [s for s in range(B) if s not in centres]:
            v = valbuf[s, :, :]
            v = jnp.concatenate(
                [jnp.where(lane < NJ, v, 0.0), jnp.where(lane < NJ, 0.0, v), jnp.zeros((2, LANES), f32)],
                axis=0,
            )
            a = v.astype(jnp.bfloat16).astype(f32)
            rest = v - a
            b = rest.astype(jnp.bfloat16).astype(f32)
            parts = jnp.concatenate([a, b, rest - b], axis=0).astype(jnp.bfloat16)
            total = total + lax.dot_general(
                parts, hits[s, :, :], (((1,), (1,)), ((), ())), preferred_element_type=f32
            )
        return total

    spot = lax.rem(mine, half)

    def differ(p, q):
        out = 0
        for b in range(half.bit_length() - 1):
            one = lax.rem(lax.div(p, 1 << b) + lax.div(q, 1 << b), 2)
            out = out + (1 << b) * one
        return out

    def near_tile(i):
        return half - 1 - i + upper * (1 + 2 * i)

    def far_tile(i):
        outer = (1 - upper) * (half - 1)
        turn = differ(spot, outer)
        if i < half - 1:
            turn = i + lax.div(i + half - turn, half)
        return (1 - upper) * half + differ(spot, turn)

    wall_first()
    for copy in j_copies[3 * B // 16 : B // 2]:
        copy.start()
    halo_recv(0)
    for u in range(half):
        first_step(u)
    wall_second()
    halo_recv(1)
    first_step(half)
    for u in range(half + 1, T):
        first_step(u)
    gather_hits()
    total = sum_nodes(0, jnp.zeros((3 * SUB, NODE_DEV), f32))
    for i in range(half - 1):
        second_step(near_tile(i))
    for i in range(half - 1):
        second_step(far_tile(i))
    second_step(near_tile(half - 1))
    second_step(far_tile(half - 1))
    total = sum_nodes(1, total)
    summed = total[0:SUB] + total[SUB : 2 * SUB] + total[2 * SUB :]
    sens[...] = summed[0:6].reshape(6, 1, NODE_DEV)
    await_bytes(jsend.at[pl.ds(0, B - 1)], j_s)
    await_bytes(jw_send.at[pl.ds(0, B - 1)], jw_s)
    await_bytes(idbuf.at[pl.ds(0, B - 1)], i_s)
    await_bytes(valbuf.at[pl.ds(0, B - 1)], v_s)
    for k in range(2):
        await_bytes(rim_send.at[k], r_s.at[k])
        await_bytes(wall, q_s.at[k])
    beside_sent(code0, h_s)
    beside_sent(code1, g_s)
    beside_sent(wall, w_s)


def hand_over(adj, sens, adj_out, sens_out, out_s):
    outs = [pltpu.make_async_copy(adj, adj_out, out_s.at[0]), pltpu.make_async_copy(sens, sens_out, out_s.at[1])]
    for copy in outs:
        copy.start()
    for copy in outs:
        copy.wait()


def body(B, passes, jac_blocks, psi_start, source, pseudo_step, dissipation, freq_volume,
         normals, face_owner, face_slot):
    _, _, planes_all, cells = jac_blocks.shape
    NJ, NK = psi_start.shape[3:]
    phase_angle = 2.0 * math.pi * ND * passes / BLADES
    R = cells // LANES
    rows = 25 * R
    pitch = -(-rows // SUB) * SUB
    faces = face_slot.shape[1]
    T = NJ // SUB
    f32 = jnp.float32
    i16 = jnp.int16
    bf16 = jnp.bfloat16
    field, plane = (10, NJ, NK), (NJ, NK)
    coded, scaled = (T, 10 * SUB, NK), (T, 10 * SUB + 2, NK)
    hbm = pl.BlockSpec(memory_space=pl.ANY)
    vm = pl.BlockSpec(memory_space=pltpu.VMEM)
    dma = pltpu.SemaphoreType.DMA
    adj, sens = pl.pallas_call(
        functools.partial(kernel, B, passes, phase_angle),
        out_shape=(
            pltpu.VMEM(field, f32),
            pltpu.VMEM((6, 1, NODE_DEV), f32),
        ),
        in_specs=[hbm] * 9,
        out_specs=(vm, vm),
        scratch_shapes=[
            pltpu.VMEM((25, planes_all, cells), bf16),
            pltpu.VMEM(field, f32),
            pltpu.VMEM(plane, f32),
            pltpu.VMEM(plane, f32),
            pltpu.VMEM(plane, f32),
            pltpu.VMEM((3, 1, faces), f32),
            pltpu.VMEM((1, faces), jnp.int32),
            pltpu.VMEM((1, faces), jnp.int32),
            pltpu.VMEM((planes_all * pitch, LANES), f32),
            pltpu.VMEM((planes_all, rows, LANES), bf16),
            pltpu.VMEM((planes_all, rows, LANES), bf16),
            pltpu.VMEM((T, 25 * SUB, LANES), f32),
            pltpu.VMEM((10, NJ + 2 * SUB, NK), f32),
            pltpu.VMEM((10, NJ + 2 * SUB, NK), f32),
            pltpu.VMEM(coded, i16),
            pltpu.VMEM(coded, i16),
            pltpu.VMEM(coded, i16),
            pltpu.VMEM(scaled, i16),
            pltpu.VMEM(scaled, i16),
            pltpu.VMEM(scaled, i16),
            pltpu.VMEM((2, 2, 2 * SUB, NK), f32),
            pltpu.VMEM((2, 2, 2 * SUB, NK), f32),
            pltpu.VMEM((SUB, LANES), f32),
            pltpu.VMEM((2, LANES, LANES), f32),
            pltpu.VMEM((LANES, LANES), f32),
            pltpu.VMEM((LANES, LANES), f32),
            pltpu.VMEM((32, LANES), f32),
            pltpu.VMEM((planes_all, 2, LANES), f32),
            pltpu.VMEM((planes_all, 2, LANES), f32),
            pltpu.VMEM((2, 2 * SUB, LANES), f32),
            pltpu.VMEM((2, 2 * SUB, LANES), f32),
            pltpu.VMEM((2, 2 * SUB, LANES), f32),
            pltpu.VMEM((2, 2, 2 * SUB, LANES), f32),
            pltpu.VMEM((B, 1, LANES), f32),
            pltpu.VMEM((B, 3, LANES), f32),
            pltpu.VMEM((B, NODE_DEV, LANES), bf16),
            dma((9,)),
            dma, dma((T,)),
            dma, dma,
            dma, dma,
            dma, dma((2,)),
            dma((2,)), dma((2, 2)),
            dma((2,)), dma((2, T)),
            dma((2,)), dma((2, 2)),
            dma((2,)), dma((2, 2)),
            dma((2,)), dma((2, 2)),
        ],
        compiler_params=pltpu.CompilerParams(collective_id=0, has_side_effects=True),
        name="flutter",
    )(jac_blocks[0], psi_start[0, :, 0], source[0, :, 0], pseudo_step[0, 0], dissipation[0, 0],
      freq_volume[0, 0], normals[0], face_owner[:, :, 0], face_slot)
    adj = pltpu.with_memory_space_constraint(adj, pltpu.VMEM)
    sens = pltpu.with_memory_space_constraint(sens, pltpu.VMEM)
    adj, sens = pl.pallas_call(
        hand_over,
        out_shape=(
            jax.ShapeDtypeStruct(field, f32),
            jax.ShapeDtypeStruct((6, 1, NODE_DEV), f32),
        ),
        in_specs=[vm, vm],
        out_specs=(hbm, hbm),
        scratch_shapes=[
            dma((2,)),
        ],
        name="hand_over",
    )(adj, sens)
    return adj[None, :, None], jnp.transpose(sens, (1, 0, 2))


def solution(mesh):
    placed = (
        P("passage", None, None, "brick"),
        P("passage", None, "brick", None, None),
        P("passage", None, "brick", None, None),
        P("passage", "brick", None, None),
        P("passage", "brick", None, None),
        P("passage", "brick", None, None),
        P("passage", None, "brick", None),
        P("passage", "brick", None),
        P("passage", "brick"),
    )
    return jax.shard_map(
        functools.partial(body, mesh.shape["brick"], mesh.shape["passage"]),
        mesh=mesh,
        in_specs=placed,
        out_specs=(P("passage", None, "brick", None, None), P("passage", None, "brick")),
        check_vma=False,
    )
```
